32 devices in a mesh: chan: 8 (over z, x), grp: 4 (over y, core).
Axes of the slice: x: 2, y: 2, z: 4, core: 2. Of those that a mesh axis runs over, the one named last changes fastest.
Arguments:
- voltage_real: bfloat16 [512, 4, 2, 256, 128], P('chan', 'grp'), may hold values from -6 to 6
- voltage_imag: bfloat16 [512, 4, 2, 256, 128], P('chan', 'grp'), may hold values from -6 to 6
- gain_real: float32 [512, 4, 2, 256], P('chan', 'grp'), may hold values from -3 to 3
- gain_imag: float32 [512, 4, 2, 256], P('chan', 'grp'), may hold values from -3 to 3
- channel_mask: int32 [8192], replicated, may hold values 0 or 1
- beam_owner: int32 [4, 256], P('grp'), may hold values from 0 to 255, each once within a row
Outputs:
- flagged: bfloat16 [2, 1024, 65536], P(None, ('chan', 'grp'))
- common_mode: float32 [65536], P(('chan', 'grp'))
The draws below stay inside these ranges and needn't reach their ends.
Inputs may be any that keep to these rules, and one draw needn't show every extreme that they name: Each row of beam_owner names every number of 0 to 255 once.
All inputs are finite; a program needn't handle non-finite values.
Results may differ from the reference program's by a relative error of at most 0.0015.
The reference program's roundings to bfloat16 on the way (of `calibrated` and `formed`) count: a program that leaves them out, or rounds other values in their place, can miss the bound.
Values may be sent and summed in bfloat16 or wider, within the bound.
No kernel may reach another device: no remote copies, remote signals or barrier semaphores. Data moves between devices by JAX's collectives and lax.ppermute only.
A program may use at most 256 MiB of HBM per device.

```python
import math
import jax
import jax.numpy as jnp
from jax import lax

FEEDS_NS = 256
CYL = 4
POL = 2
COARSE = 512
UP = 16
SAMPLES = 128
FINE = 8192
BEAMS = 1024
NS_QUARTER = 64
OWN_BEAMS = 32


def touch_ends(result, key, low, largest):
    longest = result.shape.index(max(result.shape))
    spots = []
    for shift in (0, 1):
        where = [jax.random.randint(jax.random.fold_in(key, axis), (), 0, length) for axis, length in enumerate(result.shape)]
        where[longest] = (where[longest] + shift) % result.shape[longest]
        spots.append(tuple(where))
    return result.at[spots[0]].set(low).at[spots[1]].set(largest)


def block_scale(key, dims, pieces, smallest, largest):
    factor_of, own = 1.0, jax.random.fold_in(key, 6)
    for axis_at, blocks in pieces:
        draws = jnp.exp(jax.random.uniform(jax.random.fold_in(own, axis_at), (blocks,), jnp.float32, smallest / len(pieces), largest / len(pieces)))
        factor_of = factor_of * jnp.repeat(draws, dims[axis_at] // blocks).reshape([-1 if axis == axis_at else 1 for axis in range(len(dims))])
    return factor_of


def noise(rng, dims, spread, reach, split=(), kind=jnp.bfloat16):
    result = jax.random.normal(rng, dims, jnp.float32) * spread
    if len(split) > 0:
        result = block_scale(rng, dims, split, -0.22, 0.18) * result
    return jnp.clip(result, min=-reach, max=reach).astype(kind)


def setup_inputs(seed: int = 0) -> dict:
    key_list = jax.random.split(jax.random.key(seed), 7)
    voltage_real = noise(key_list[0], (COARSE, CYL, POL, FEEDS_NS, SAMPLES), 1.0, 6.0, ((0, 8), (1, 4)))
    voltage_imag = noise(key_list[1], (COARSE, CYL, POL, FEEDS_NS, SAMPLES), 1.0, 6.0, ((0, 8), (1, 4)))
    gain_real = noise(key_list[2], (COARSE, CYL, POL, FEEDS_NS), 0.5, 3.0, ((0, 8), (1, 4)), jnp.float32)
    gain_imag = noise(key_list[3], (COARSE, CYL, POL, FEEDS_NS), 0.5, 3.0, ((0, 8), (1, 4)), jnp.float32)
    channel_mask = touch_ends((jax.random.randint(key_list[4], (FINE,), 0, 8) < 7).astype(jnp.int32), jax.random.fold_in(key_list[4], 1), 0, 1)
    beam_owner = jax.vmap(lambda own: jax.random.permutation(own, FEEDS_NS))(jax.random.split(key_list[5], CYL)).reshape((CYL, FEEDS_NS)).astype(jnp.int32)
    return {"voltage_real": voltage_real, "voltage_imag": voltage_imag, "gain_real": gain_real, "gain_imag": gain_imag, "channel_mask": channel_mask, "beam_owner": beam_owner}


epsilon = 1e-05

def beam_table(feed_count):
    counter = jnp.arange(feed_count, dtype=jnp.int32)
    phases = counter[:, None] * counter[None, :] % feed_count
    angles = phases.astype(jnp.float32) * (-2.0 * math.pi / feed_count)
    factor = 1.0 / math.sqrt(feed_count)
    cosine = jnp.cos(angles) * factor
    sines = jnp.sin(angles) * factor
    real_rows = jnp.stack([cosine, -sines], axis=1)
    imaginary_rows = jnp.stack([sines, cosine], axis=1)
    return jnp.stack([real_rows, imaginary_rows], axis=0).astype(jnp.bfloat16)

def stokes_table(column_count, up_count):
    columns = jnp.arange(column_count, dtype=jnp.int32)
    spectral = jnp.arange(up_count, dtype=jnp.int32)
    column_phase = columns[:, None] * columns[None, :] % column_count
    spectral_phase = spectral[:, None] * spectral[None, :] % up_count
    phases = column_phase[:, None, :, None] * up_count + spectral_phase[None, :, None, :] * column_count
    angles = phases.astype(jnp.float32) * (-2.0 * math.pi / (column_count * up_count))
    factor = 1.0 / math.sqrt(column_count * up_count)
    cosine = jnp.cos(angles) * factor
    sines = jnp.sin(angles) * factor
    real_rows = jnp.stack([cosine, -sines], axis=2)
    imaginary_rows = jnp.stack([sines, cosine], axis=2)
    return jnp.stack([real_rows, imaginary_rows], axis=0)

def calibrate(voltage_real, voltage_imag, gain_real, gain_imag):
    real_gain = gain_real[..., None]
    imaginary_gain = gain_imag[..., None]
    real_volt = voltage_real.astype(jnp.float32)
    imaginary_volt = voltage_imag.astype(jnp.float32)
    real_part = real_gain * real_volt - imaginary_gain * imaginary_volt
    imaginary_part = real_gain * imaginary_volt + imaginary_gain * real_volt
    return jnp.stack([real_part, imaginary_part], axis=-3).astype(jnp.bfloat16)

def beamform(calibrated, weights):
    formed = jnp.einsum('amrn,cyprns->cypams', weights, calibrated, preferred_element_type=jnp.float32)
    return formed.astype(jnp.bfloat16)

def detect_stokes(formed, weights):
    column_count, pol_count, parts_count, beam_count, sample_count = formed.shape
    up_count = weights.shape[2]
    frame_count = sample_count // up_count
    shaped = formed.reshape(column_count, pol_count, parts_count, beam_count, frame_count, up_count).astype(jnp.float32)
    fields = jnp.einsum('aekrqu,qprmfu->paemkf', weights, shaped, precision=lax.Precision.HIGHEST)
    first_real = fields[0, 0]
    first_imaginary = fields[0, 1]
    second_real = fields[1, 0]
    second_imaginary = fields[1, 1]
    intensity = first_real * first_real + first_imaginary * first_imaginary + second_real * second_real + second_imaginary * second_imaginary
    circular = 2.0 * (first_imaginary * second_real - first_real * second_imaginary)
    stacked = jnp.stack([intensity, circular]).reshape(2, weights.shape[1], beam_count, sample_count)
    return stacked.astype(jnp.bfloat16)

def soft_flag(spectra, common, mask_grid):
    coarse_count, stokes_count, beam_count, sample_count = spectra.shape
    up_count = mask_grid.shape[1]
    frame_count = sample_count // up_count
    cleaned = (spectra[:, 0].astype(jnp.float32) - common[:, None, :]).reshape(coarse_count, beam_count, up_count, frame_count)
    circular = spectra[:, 1].astype(jnp.float32).reshape(coarse_count, beam_count, up_count, frame_count)
    power = lax.optimization_barrier(jnp.mean(cleaned * cleaned, axis=3))
    level = lax.optimization_barrier(jnp.mean(power, axis=(0, 2))) + epsilon
    weights = mask_grid[:, None, :] / (1.0 + power / (2.0 * level[None, :, None]))
    flagged = jnp.stack([cleaned * weights[..., None], circular * weights[..., None]])
    flagged = jnp.transpose(flagged, (0, 2, 1, 3, 4)).reshape(2, beam_count, coarse_count * sample_count)
    return flagged.astype(jnp.bfloat16)

def reference(voltage_real, voltage_imag, gain_real, gain_imag, channel_mask, beam_owner):
    feed_weights = beam_table(FEEDS_NS)
    column_weights = stokes_table(CYL, UP)

    def per_channel(channel):
        calibrated = calibrate(voltage_real[channel][None], voltage_imag[channel][None], gain_real[channel][None], gain_imag[channel][None])
        formed = beamform(calibrated, feed_weights)
        return detect_stokes(formed[0], column_weights)
    stokes = lax.map(per_channel, jnp.arange(COARSE, dtype=jnp.int32))
    common = lax.optimization_barrier(jnp.sum(stokes[:, 0], axis=(1, 2), dtype=jnp.float32)) / BEAMS
    mask_grid = channel_mask.reshape(COARSE, UP).astype(jnp.float32)
    outputs = jnp.arange(BEAMS, dtype=jnp.int32)
    block_index = outputs // OWN_BEAMS
    group_index = block_index % CYL
    position = block_index // CYL * OWN_BEAMS + outputs % OWN_BEAMS
    local_beam = beam_owner[group_index, position]
    column_index = local_beam // NS_QUARTER
    north_index = group_index * NS_QUARTER + local_beam % NS_QUARTER

    def per_beam(pair):
        column, north = pair
        spectra = stokes[:, :, column, north][:, :, None, :]
        return soft_flag(spectra, common, mask_grid)[:, 0]
    flagged = lax.map(per_beam, (column_index, north_index))
    return (jnp.transpose(flagged, (1, 0, 2)), common.reshape(-1))
```

```python
import math

import jax
import jax.numpy as jnp
import numpy as np
from jax import lax
from jax.experimental import pallas as pl
from jax.experimental.pallas import tpu as pltpu
from jax.sharding import PartitionSpec as P

UP = 16
CHUNKS = 8
AHEAD = 1

epsilon = 1e-05


def beam_table(feed_count):
    counter = jnp.arange(feed_count, dtype=jnp.int32)
    phases = counter[:, None] * counter[None, :] % feed_count
    angles = phases.astype(jnp.float32) * (-2.0 * math.pi / feed_count)
    factor = 1.0 / math.sqrt(feed_count)
    cosine = jnp.cos(angles) * factor
    sines = jnp.sin(angles) * factor
    real_rows = jnp.concatenate([cosine, -sines], axis=1)
    imaginary_rows = jnp.concatenate([sines, cosine], axis=1)
    return jnp.concatenate([real_rows, imaginary_rows], axis=0).astype(jnp.bfloat16)


def spectral_tables(up_count, frame_count, column_count):
    spectral = np.arange(up_count)
    angles = (spectral[:, None] * spectral[None, :] % up_count) * (-2.0 * math.pi / up_count)
    factor = 1.0 / math.sqrt(column_count * up_count)
    cosine, sines = np.cos(angles) * factor, np.sin(angles) * factor
    same = np.eye(frame_count)
    sample_count = frame_count * up_count

    def spread(entries):
        return np.einsum("uk,tv->tukv", entries, same).reshape(sample_count, sample_count)

    table = np.block([[spread(cosine), spread(sines)], [-spread(sines), spread(cosine)]])
    table = table.astype(np.float32)
    high = table.astype(jnp.bfloat16)
    low = (table - high.astype(np.float32)).astype(jnp.bfloat16)
    return high, low


def form_kernel(after_ref, table_ref, gain_real_ref, gain_imag_ref, real_ref, imag_ref, *out_refs):
    channels, pols, _, beams, samples = out_refs[0].shape
    gains_real, gains_imag = gain_real_ref[0].T, gain_imag_ref[0].T
    for c in range(channels):
        columns = []
        for p in range(pols):
            j = c * pols + p
            gain_real, gain_imag = gains_real[:, j : j + 1], gains_imag[:, j : j + 1]
            real = real_ref[c, 0, p].astype(jnp.float32)
            imag = imag_ref[c, 0, p].astype(jnp.float32)
            real_part = (gain_real * real - gain_imag * imag).astype(jnp.bfloat16)
            imag_part = (gain_real * imag + gain_imag * real).astype(jnp.bfloat16)
            columns.append(jnp.concatenate([real_part, imag_part], axis=0))
        calibrated = jnp.concatenate(columns, axis=1)
        formed = jnp.dot(table_ref[...], calibrated, preferred_element_type=jnp.float32)
        formed = formed.astype(jnp.bfloat16)
        for p in range(pols):
            for r, out_ref in enumerate(out_refs):
                for a in range(2):
                    row = (r * 2 + a) * beams
                    out_ref[c, p, a] = formed[row : row + beams, p * samples : (p + 1) * samples]


def detect_kernel(me_ref, after_ref, before_ref, high_ref, low_ref, order_ref, *refs):
    formed_refs, (out_ref, sum_ref, rows_ref) = refs[:-3], refs[-3:]
    columns = len(formed_refs)
    channels, pols, _, beams, samples = formed_refs[0].shape
    owners, _, own, _ = out_ref.shape
    for c in range(channels):
        for r, formed_ref in enumerate(formed_refs):
            y = me_ref[0] ^ r
            for p in range(pols):
                for a in range(2):
                    rows_ref[p, y, :, a * samples : (a + 1) * samples] = formed_ref[c, p, a]
        rows = rows_ref[...].reshape(pols * columns * beams, 2 * samples)
        spectra = jnp.dot(rows, high_ref[...], preferred_element_type=jnp.float32) + jnp.dot(
            rows, low_ref[...], preferred_element_type=jnp.float32
        )
        real, imag = [], []
        for p in range(pols):
            g = [spectra[(p * columns + y) * beams :][:beams] for y in range(columns)]
            even_sum, even_diff = g[0] + g[2], g[0] - g[2]
            odd_sum, odd_diff = g[1] + g[3], g[1] - g[3]
            zero, two = even_sum + odd_sum, even_sum - odd_sum
            dr, di = even_diff[:, :samples], even_diff[:, samples:]
            qr, qi = odd_diff[:, :samples], odd_diff[:, samples:]
            real.append([zero[:, :samples], dr + qi, two[:, :samples], dr - qi])
            imag.append([zero[:, samples:], di - qr, two[:, samples:], di + qr])
        stokes, total = [], None
        for e in range(columns):
            xr, xi, yr, yi = real[0][e], imag[0][e], real[1][e], imag[1][e]
            intensity = (xr * xr + xi * xi + yr * yr + yi * yi).astype(jnp.bfloat16)
            circular = (2.0 * (xi * yr - xr * yi)).astype(jnp.bfloat16)
            stokes.append(jnp.concatenate([intensity, circular], axis=1))
            part = intensity.astype(jnp.float32)
            total = part if total is None else total + part
        sum_ref[0, c : c + 1, :] = jnp.sum(total, axis=0, keepdims=True)
        ordered = jnp.dot(
            order_ref[...], jnp.concatenate(stokes, axis=0), preferred_element_type=jnp.float32
        )
        for d in range(owners):
            out_ref[d, c] = ordered[d * own : (d + 1) * own].astype(jnp.bfloat16)


def flag_kernel(frame_count, group_ref, common_ref, mask_ref, *refs):
    chunk_refs, out_ref, power_ref = refs[:-2], refs[-2], refs[-1]
    sources, per_chunk, beams, width = chunk_refs[0].shape
    samples = width // 2
    local = per_chunk * len(chunk_refs)

    def measure(s, level):
        for i, chunk_ref in enumerate(chunk_refs):
            first = s * local + i * per_chunk
            common = common_ref[pl.ds(first, per_chunk)]
            cleaned = chunk_ref[s, :, :, :samples].astype(jnp.float32) - common
            squares = (cleaned * cleaned).reshape(per_chunk * beams, samples)
            high = squares.astype(jnp.bfloat16)
            low = (squares - high.astype(jnp.float32)).astype(jnp.bfloat16)
            power = jnp.dot(high, group_ref[...], preferred_element_type=jnp.float32) + jnp.dot(
                low, group_ref[...], preferred_element_type=jnp.float32
            )
            power = power.reshape(per_chunk, beams, samples)
            power_ref[pl.ds(first, per_chunk)] = power
            level = level + jnp.sum(power, axis=0)
        return level

    level = lax.fori_loop(0, sources, measure, jnp.zeros((beams, samples), jnp.float32))
    level = jnp.sum(level, axis=1, keepdims=True) / float(sources * local * samples) + epsilon
    scale = jnp.broadcast_to(0.5 / level, (beams, samples))

    def flag(s, carry):
        for i, chunk_ref in enumerate(chunk_refs):
            for c in range(per_chunk):
                channel = s * local + i * per_chunk + c
                row = chunk_ref[s, c].astype(jnp.float32)
                cleaned = row[:, :samples] - common_ref[channel]
                weight = mask_ref[channel] / (1.0 + power_ref[channel] * scale)
                where = pl.ds(pl.multiple_of(channel * samples, samples), samples)
                out_ref[0, :, where] = (cleaned * weight).astype(jnp.bfloat16)
                out_ref[1, :, where] = (row[:, samples:] * weight).astype(jnp.bfloat16)
        return carry

    lax.fori_loop(0, sources, flag, 0)


def whole_spec(array):
    return pl.BlockSpec(array.shape, lambda *_: (0,) * array.ndim)


def form(after, table, gains, volts, chunk, per_chunk, step, groups):
    real, imag = volts
    _, _, pols, feeds, samples = real.shape
    steps = per_chunk // step
    gain_spec = pl.BlockSpec((1, *gains[0].shape[1:]), lambda i: (chunk * steps + i, 0, 0))
    volt_spec = pl.BlockSpec(
        (step, 1, pols, feeds, samples), lambda i: (chunk * steps + i, 0, 0, 0, 0)
    )
    beams = feeds // groups
    return pl.pallas_call(
        form_kernel,
        grid=(steps,),
        in_specs=[pl.BlockSpec(memory_space=pl.ANY), whole_spec(table), gain_spec, gain_spec, volt_spec, volt_spec],
        out_specs=[pl.BlockSpec((step, pols, 2, beams, samples), lambda i: (i, 0, 0, 0, 0))]
        * groups,
        out_shape=[jax.ShapeDtypeStruct((per_chunk, pols, 2, beams, samples), jnp.bfloat16)]
        * groups,
        cost_estimate=pl.CostEstimate(
            flops=per_chunk * pols * 8 * feeds * feeds * samples,
            bytes_accessed=per_chunk * pols * feeds * samples * 8,
            transcendentals=0,
        ),
        compiler_params=pltpu.CompilerParams(vmem_limit_bytes=60 << 20),
        name="form",
    )(after, table, *gains, real, imag)


def detect(me, tables, order, formed, after, step, owners):
    columns = len(formed)
    per_chunk, pols, _, beams, samples = formed[0].shape
    steps = per_chunk // step
    own = columns * beams // owners
    return pl.pallas_call(
        detect_kernel,
        grid=(steps,),
        in_specs=[
            pl.BlockSpec(memory_space=pltpu.SMEM),
            pl.BlockSpec(memory_space=pl.ANY),
            pl.BlockSpec(memory_space=pl.ANY),
            *[whole_spec(table) for table in tables],
            whole_spec(order),
            *[pl.BlockSpec((step, pols, 2, beams, samples), lambda i: (i, 0, 0, 0, 0))] * columns,
        ],
        out_specs=[
            pl.BlockSpec((owners, step, own, 2 * samples), lambda i: (0, i, 0, 0)),
            pl.BlockSpec((1, step, samples), lambda i: (i, 0, 0)),
        ],
        out_shape=[
            jax.ShapeDtypeStruct((owners, per_chunk, own, 2 * samples), jnp.bfloat16),
            jax.ShapeDtypeStruct((steps, step, samples), jnp.float32),
        ],
        scratch_shapes=[pltpu.VMEM((pols, columns, beams, 2 * samples), jnp.bfloat16)],
        cost_estimate=pl.CostEstimate(
            flops=per_chunk * columns * beams * samples * samples * 24,
            bytes_accessed=per_chunk * columns * beams * samples * 12,
            transcendentals=0,
        ),
        compiler_params=pltpu.CompilerParams(vmem_limit_bytes=60 << 20),
        name="detect",
    )(me, *after, *tables, order, *formed)


def soft_flag(owned, common, mask, frame_count):
    sources, per_chunk, own, width = owned[0].shape
    samples = width // 2
    channels = common.shape[0]
    block = 16 if own % 16 == 0 else own
    group = np.kron(np.eye(samples // frame_count), np.ones((frame_count, frame_count)))
    group = jnp.asarray(group / frame_count, jnp.bfloat16)
    return pl.pallas_call(
        lambda *refs: flag_kernel(frame_count, *refs),
        grid=(own // block,),
        in_specs=[
            whole_spec(group),
            whole_spec(common),
            whole_spec(mask),
            *[
                pl.BlockSpec((sources, per_chunk, block, width), lambda i: (0, 0, i, 0))
                for _ in owned
            ],
        ],
        out_specs=pl.BlockSpec((2, block, channels * samples), lambda i: (0, i, 0)),
        out_shape=jax.ShapeDtypeStruct((2, own, channels * samples), jnp.bfloat16),
        scratch_shapes=[pltpu.VMEM((channels, block, samples), jnp.float32)],
        cost_estimate=pl.CostEstimate(
            flops=channels * own * samples * samples * 4,
            bytes_accessed=channels * own * samples * 8,
            transcendentals=0,
        ),
        compiler_params=pltpu.CompilerParams(vmem_limit_bytes=60 << 20),
        name="flag",
    )(group, common, mask, *owned)


def body(voltage_real, voltage_imag, gain_real, gain_imag, channel_mask, beam_owner):
    local, _, pols, feeds, samples = voltage_real.shape
    frame_count = samples // UP
    owners, groups = lax.axis_size("chan"), lax.axis_size("grp")
    channels = local * owners
    per_chunk = max(local // CHUNKS, 1)
    chunks = local // per_chunk
    step = math.gcd(per_chunk, 2)

    def rows_of(gain):
        rows = gain.reshape(local // step, step * pols, feeds)
        return jnp.pad(rows, ((0, 0), (0, -rows.shape[1] % 8), (0, 0)))

    gains = (rows_of(gain_real), rows_of(gain_imag))
    mine = lax.axis_index("grp")
    table = beam_table(feeds).reshape(2, groups, feeds // groups, 2 * feeds)
    table = jnp.stack([table[:, mine ^ r] for r in range(groups)]).reshape(2 * feeds, 2 * feeds)
    me = mine.astype(jnp.int32).reshape(1)
    tables = [jnp.asarray(one) for one in spectral_tables(UP, frame_count, groups)]
    slots = beam_owner.shape[1]
    order = (beam_owner[0][:, None] == jnp.arange(slots, dtype=jnp.int32)[None, :]).astype(
        jnp.bfloat16
    )
    mask = jnp.repeat(channel_mask.astype(jnp.float32), frame_count).reshape(channels, 1, samples)
    volts = (voltage_real, voltage_imag)
    turned, owned, sums = [], [], []
    after = me
    for chunk in range(chunks + AHEAD):
        if chunk < chunks:
            formed = form(after, table, gains, volts, chunk, per_chunk, step, groups)
            turned.append(
                [
                    lax.ppermute(one, "grp", [(g, g ^ r) for g in range(groups)]) if r else one
                    for r, one in enumerate(formed)
                ]
            )
            after = formed[0]
        if chunk >= AHEAD:
            blocks = turned[chunk - AHEAD]
            before = owned[-2:-1] or [me]
            stokes, part = detect(me, tables, order, blocks, [after, before[0]], step, owners)
            owned.append(lax.all_to_all(stokes, "chan", split_axis=0, concat_axis=0, tiled=True))
            sums.append(part.reshape(per_chunk, samples))
            after = stokes
    partial = jnp.concatenate(sums, axis=0)
    gathered = lax.all_gather(partial, ("chan", "grp"), axis=0)
    common = jnp.sum(gathered.reshape(owners, groups, local, samples), axis=1)
    common = common.reshape(channels, samples) / float(feeds * groups)
    flagged = soft_flag(owned, common.reshape(channels, 1, samples), mask, frame_count)
    flattened = common.reshape(-1)
    piece = flattened.shape[0] // (owners * groups)
    position = lax.axis_index("chan") * groups + lax.axis_index("grp")
    return (flagged, lax.dynamic_slice_in_dim(flattened, position * piece, piece))


def solution(mesh):
    in_specs = (
        P("chan", "grp", None, None, None),
        P("chan", "grp", None, None, None),
        P("chan", "grp", None, None),
        P("chan", "grp", None, None),
        P(),
        P("grp", None),
    )
    out_specs = (P(None, ("chan", "grp"), None), P(("chan", "grp")))
    return jax.shard_map(body, mesh=mesh, in_specs=in_specs, out_specs=out_specs, check_vma=False)
```

```python
import math

import jax
import jax.numpy as jnp
import numpy as np
from jax import lax
from jax.experimental import pallas as pl
from jax.experimental.pallas import tpu as pltpu
from jax.sharding import PartitionSpec as P

UP = 16
SHARES = (2, 3, 4, 6, 8, 9)
DETECT_FLOPS = 30_000_000_000

epsilon = 1e-05


def beam_table(feed_count):
    counter = jnp.arange(feed_count, dtype=jnp.int32)
    phases = counter[:, None] * counter[None, :] % feed_count
    angles = phases.astype(jnp.float32) * (-2.0 * math.pi / feed_count)
    factor = 1.0 / math.sqrt(feed_count)
    cosine = jnp.cos(angles) * factor
    sines = jnp.sin(angles) * factor
    real_rows = jnp.concatenate([cosine, -sines], axis=1)
    imaginary_rows = jnp.concatenate([sines, cosine], axis=1)
    return jnp.concatenate([real_rows, imaginary_rows], axis=0).astype(jnp.bfloat16)


def spectral_tables(up_count, frame_count, column_count):
    spectral = np.arange(up_count)
    angles = (spectral[:, None] * spectral[None, :] % up_count) * (-2.0 * math.pi / up_count)
    factor = 1.0 / math.sqrt(column_count * up_count)
    cosine, sines = np.cos(angles) * factor, np.sin(angles) * factor
    same = np.eye(frame_count)
    sample_count = frame_count * up_count

    def spread(entries):
        return np.einsum("uk,tv->tukv", entries, same).reshape(sample_count, sample_count)

    table = np.block([[spread(cosine), spread(sines)], [-spread(sines), spread(cosine)]])
    table = table.astype(np.float32)
    high = table.astype(jnp.bfloat16)
    low = (table - high.astype(np.float32)).astype(jnp.bfloat16)
    return high, low


def form_kernel(after_ref, table_ref, gain_real_ref, gain_imag_ref, real_ref, imag_ref, *out_refs):
    channels, pols, _, beams, samples = out_refs[0].shape
    gains_real, gains_imag = gain_real_ref[0].T, gain_imag_ref[0].T
    for c in range(channels):
        columns = []
        for p in range(pols):
            j = c * pols + p
            gain_real, gain_imag = gains_real[:, j : j + 1], gains_imag[:, j : j + 1]
            real = real_ref[c, 0, p].astype(jnp.float32)
            imag = imag_ref[c, 0, p].astype(jnp.float32)
            real_part = (gain_real * real - gain_imag * imag).astype(jnp.bfloat16)
            imag_part = (gain_real * imag + gain_imag * real).astype(jnp.bfloat16)
            columns.append(jnp.concatenate([real_part, imag_part], axis=0))
        calibrated = jnp.concatenate(columns, axis=1)
        formed = jnp.dot(table_ref[...], calibrated, preferred_element_type=jnp.float32)
        formed = formed.astype(jnp.bfloat16)
        for p in range(pols):
            for r, out_ref in enumerate(out_refs):
                for a in range(2):
                    row = (r * 2 + a) * beams
                    out_ref[c, p, a] = formed[row : row + beams, p * samples : (p + 1) * samples]


def detect_kernel(me_ref, after_ref, before_ref, high_ref, low_ref, order_ref, *refs):
    formed_refs, (out_ref, sum_ref, rows_ref) = refs[:-3], refs[-3:]
    owners, channels, own, _ = out_ref.shape
    columns = len(formed_refs)
    _, pols, _, beams, samples = formed_refs[0].shape
    for c in range(channels):
        for r, formed_ref in enumerate(formed_refs):
            y = me_ref[0] ^ r
            for p in range(pols):
                for a in range(2):
                    rows_ref[p, y, :, a * samples : (a + 1) * samples] = formed_ref[c, p, a]
        rows = rows_ref[...].reshape(pols * columns * beams, 2 * samples)
        spectra = jnp.dot(rows, high_ref[...], preferred_element_type=jnp.float32) + jnp.dot(
            rows, low_ref[...], preferred_element_type=jnp.float32
        )
        real, imag = [], []
        for p in range(pols):
            g = [spectra[(p * columns + y) * beams :][:beams] for y in range(columns)]
            even_sum, even_diff = g[0] + g[2], g[0] - g[2]
            odd_sum, odd_diff = g[1] + g[3], g[1] - g[3]
            zero, two = even_sum + odd_sum, even_sum - odd_sum
            dr, di = even_diff[:, :samples], even_diff[:, samples:]
            qr, qi = odd_diff[:, :samples], odd_diff[:, samples:]
            real.append([zero[:, :samples], dr + qi, two[:, :samples], dr - qi])
            imag.append([zero[:, samples:], di - qr, two[:, samples:], di + qr])
        stokes, total = [], None
        for e in range(columns):
            xr, xi, yr, yi = real[0][e], imag[0][e], real[1][e], imag[1][e]
            intensity = (xr * xr + xi * xi + yr * yr + yi * yi).astype(jnp.bfloat16)
            circular = (2.0 * (xi * yr - xr * yi)).astype(jnp.bfloat16)
            stokes.append(jnp.concatenate([intensity, circular], axis=1))
            part = intensity.astype(jnp.float32)
            total = part if total is None else total + part
        sum_ref[0, c : c + 1, :] = jnp.sum(total, axis=0, keepdims=True)
        ordered = jnp.dot(
            order_ref[...], jnp.concatenate(stokes, axis=0), preferred_element_type=jnp.float32
        )
        for d in range(owners):
            out_ref[d, c] = ordered[d * own : (d + 1) * own].astype(jnp.bfloat16)


def flag_kernel(group_ref, common_ref, mask_ref, *refs):
    chunk_refs, out_ref, power_ref = refs[:-2], refs[-2], refs[-1]
    sources, _, beams, width = chunk_refs[0].shape
    samples = width // 2
    sizes = [chunk_ref.shape[1] for chunk_ref in chunk_refs]
    local = sum(sizes)

    def measure(s, level):
        first = s * local
        for size, chunk_ref in zip(sizes, chunk_refs):
            common = common_ref[pl.ds(first, size)]
            cleaned = chunk_ref[s, :, :, :samples].astype(jnp.float32) - common
            squares = (cleaned * cleaned).reshape(size * beams, samples)
            high = squares.astype(jnp.bfloat16)
            low = (squares - high.astype(jnp.float32)).astype(jnp.bfloat16)
            power = jnp.dot(high, group_ref[...], preferred_element_type=jnp.float32) + jnp.dot(
                low, group_ref[...], preferred_element_type=jnp.float32
            )
            power = power.reshape(size, beams, samples)
            power_ref[pl.ds(first, size)] = power
            level = level + jnp.sum(power, axis=0)
            first = first + size
        return level

    level = lax.fori_loop(0, sources, measure, jnp.zeros((beams, samples), jnp.float32))
    level = jnp.sum(level, axis=1, keepdims=True) / float(sources * local * samples) + epsilon
    scale = jnp.broadcast_to(0.5 / level, (beams, samples))

    def flag(s, carry):
        channel = s * local
        for size, chunk_ref in zip(sizes, chunk_refs):
            for c in range(size):
                row = chunk_ref[s, c].astype(jnp.float32)
                cleaned = row[:, :samples] - common_ref[channel]
                weight = mask_ref[channel] / (1.0 + power_ref[channel] * scale)
                where = pl.ds(pl.multiple_of(channel * samples, samples), samples)
                out_ref[0, :, where] = (cleaned * weight).astype(jnp.bfloat16)
                out_ref[1, :, where] = (row[:, samples:] * weight).astype(jnp.bfloat16)
                channel = channel + 1
        return carry

    lax.fori_loop(0, sources, flag, 0)


def whole_spec(array):
    return pl.BlockSpec(array.shape, lambda *_: (0,) * array.ndim)


def form(after, table, gains, volts, first, per_chunk, step, groups):
    real, imag = volts
    _, _, pols, feeds, samples = real.shape
    steps = per_chunk // step
    gain_spec = pl.BlockSpec((1, *gains[0].shape[1:]), lambda i: (first // step + i, 0, 0))
    volt_spec = pl.BlockSpec(
        (step, 1, pols, feeds, samples), lambda i: (first // step + i, 0, 0, 0, 0)
    )
    beams = feeds // groups
    return pl.pallas_call(
        form_kernel,
        grid=(steps,),
        in_specs=[pl.BlockSpec(memory_space=pl.ANY), whole_spec(table), gain_spec, gain_spec, volt_spec, volt_spec],
        out_specs=[pl.BlockSpec((step, pols, 2, beams, samples), lambda i: (i, 0, 0, 0, 0))]
        * groups,
        out_shape=[jax.ShapeDtypeStruct((per_chunk, pols, 2, beams, samples), jnp.bfloat16)]
        * groups,
        cost_estimate=pl.CostEstimate(
            flops=1000,
            bytes_accessed=1000,
            transcendentals=0,
        ),
        compiler_params=pltpu.CompilerParams(vmem_limit_bytes=60 << 20),
        name="form",
    )(after, table, *gains, real, imag)


def detect(me, tables, order, formed, after, step, owners):
    columns = len(formed)
    per_chunk, pols, _, beams, samples = formed[0].shape
    steps = per_chunk // step
    own = columns * beams // owners
    block_spec = pl.BlockSpec((step, pols, 2, beams, samples), lambda i: (i, 0, 0, 0, 0))
    return pl.pallas_call(
        detect_kernel,
        grid=(steps,),
        in_specs=[
            pl.BlockSpec(memory_space=pltpu.SMEM),
            pl.BlockSpec(memory_space=pl.ANY),
            pl.BlockSpec(memory_space=pl.ANY),
            *[whole_spec(table) for table in tables],
            whole_spec(order),
            *[block_spec] * columns,
        ],
        out_specs=[
            pl.BlockSpec((owners, step, own, 2 * samples), lambda i: (0, i, 0, 0)),
            pl.BlockSpec((1, step, samples), lambda i: (i, 0, 0)),
        ],
        out_shape=[
            jax.ShapeDtypeStruct((owners, per_chunk, own, 2 * samples), jnp.bfloat16),
            jax.ShapeDtypeStruct((steps, step, samples), jnp.float32),
        ],
        scratch_shapes=[pltpu.VMEM((pols, columns, beams, 2 * samples), jnp.bfloat16)],
        cost_estimate=pl.CostEstimate(
            flops=DETECT_FLOPS,
            bytes_accessed=1000,
            transcendentals=0,
        ),
        compiler_params=pltpu.CompilerParams(vmem_limit_bytes=60 << 20),
        name="detect",
    )(me, *after, *tables, order, *formed)


def soft_flag(owned, common, mask, frame_count):
    sources, _, own, width = owned[0].shape
    samples = width // 2
    channels = common.shape[0]
    block = 16 if own % 16 == 0 else own
    group = np.kron(np.eye(samples // frame_count), np.ones((frame_count, frame_count)))
    group = jnp.asarray(group / frame_count, jnp.bfloat16)
    return pl.pallas_call(
        flag_kernel,
        grid=(own // block,),
        in_specs=[
            whole_spec(group),
            whole_spec(common),
            whole_spec(mask),
            *[
                pl.BlockSpec((sources, one.shape[1], block, width), lambda i: (0, 0, i, 0))
                for one in owned
            ],
        ],
        out_specs=pl.BlockSpec((2, block, channels * samples), lambda i: (0, i, 0)),
        out_shape=jax.ShapeDtypeStruct((2, own, channels * samples), jnp.bfloat16),
        scratch_shapes=[pltpu.VMEM((channels, block, samples), jnp.float32)],
        cost_estimate=pl.CostEstimate(
            flops=channels * own * samples * samples * 4,
            bytes_accessed=channels * own * samples * 8,
            transcendentals=0,
        ),
        compiler_params=pltpu.CompilerParams(vmem_limit_bytes=60 << 20),
        name="flag",
    )(group, common, mask, *owned)


def swap(one, axis, apart):
    return lax.ppermute(one, axis, [(i, i ^ apart) for i in range(lax.axis_size(axis))])


def body(voltage_real, voltage_imag, gain_real, gain_imag, channel_mask, beam_owner):
    local, _, pols, feeds, samples = voltage_real.shape
    frame_count = samples // UP
    owners, groups = lax.axis_size("chan"), lax.axis_size("grp")
    channels = local * owners
    unit = local // sum(SHARES)
    sizes = [share * unit for share in SHARES] if local == unit * sum(SHARES) else [1] * local
    chunks = len(sizes)
    firsts = [sum(sizes[:chunk]) for chunk in range(chunks)]
    step = math.gcd(*sizes, 2)

    def rows_of(gain):
        rows = gain.reshape(local // step, step * pols, feeds)
        return jnp.pad(rows, ((0, 0), (0, -rows.shape[1] % 8), (0, 0)))

    gains = (rows_of(gain_real), rows_of(gain_imag))
    mine = lax.axis_index("grp")
    table = beam_table(feeds).reshape(2, groups, feeds // groups, 2 * feeds)
    table = jnp.stack([table[:, mine ^ r] for r in range(groups)]).reshape(2 * feeds, 2 * feeds)
    me = mine.astype(jnp.int32).reshape(1)
    tables = [jnp.asarray(one) for one in spectral_tables(UP, frame_count, groups)]
    slots = beam_owner.shape[1]
    order = (beam_owner[0][:, None] == jnp.arange(slots, dtype=jnp.int32)[None, :]).astype(
        jnp.bfloat16
    )
    mask = jnp.repeat(channel_mask.astype(jnp.float32), frame_count).reshape(channels, 1, samples)
    volts = (voltage_real, voltage_imag)
    turned, owned, sums = [], [], []
    after = me
    for chunk in range(chunks + 1):
        if chunk < chunks:
            formed = form(
                after, table, gains, volts, firsts[chunk], sizes[chunk], step, groups
            )
            turned.append([swap(one, "grp", r) if r else one for r, one in enumerate(formed)])
            after = formed[0]
        if chunk > 0:
            before = owned[-2:-1] or [me]
            stokes, part = detect(
                me, tables, order, turned[chunk - 1], [after, before[0]], step, owners
            )
            owned.append(lax.all_to_all(stokes, "chan", split_axis=0, concat_axis=0, tiled=True))
            sums.append(part.reshape(sizes[chunk - 1], samples))
            after = stokes
    common = jnp.concatenate(sums, axis=0)
    for bit in range(groups.bit_length() - 1):
        common = common + swap(common, "grp", 1 << bit)
    common = common / float(feeds * groups)
    piece = local // groups
    common_piece = lax.dynamic_slice_in_dim(common, mine * piece, piece).reshape(-1)
    for bit in range(owners.bit_length() - 1):
        other = swap(common, "chan", 1 << bit)
        low = (lax.axis_index("chan") >> bit) % 2 == 0
        common = jnp.where(low, jnp.stack([common, other]), jnp.stack([other, common]))
        common = common.reshape(-1, samples)
    flagged = soft_flag(owned, common.reshape(channels, 1, samples), mask, frame_count)
    return (flagged, common_piece)


def solution(mesh):
    in_specs = (
        P("chan", "grp", None, None, None),
        P("chan", "grp", None, None, None),
        P("chan", "grp", None, None),
        P("chan", "grp", None, None),
        P(),
        P("grp", None),
    )
    out_specs = (P(None, ("chan", "grp"), None), P(("chan", "grp")))
    return jax.shard_map(body, mesh=mesh, in_specs=in_specs, out_specs=out_specs, check_vma=False)
```

```python
import math

import jax
import jax.numpy as jnp
import numpy as np
from jax import lax
from jax.experimental import pallas as pl
from jax.experimental.pallas import tpu as pltpu
from jax.sharding import PartitionSpec as P

UP = 16
SHARES = (2, 3, 4, 6, 8, 9)
DETECT_FLOPS = 1_600_000_000

epsilon = 1e-05


def beam_table(feed_count, group_count):
    counter = np.arange(feed_count)
    angles = (counter[:, None] * counter[None, :] % feed_count) * (-2.0 * math.pi / feed_count)
    factor = 1.0 / math.sqrt(feed_count)
    cosine, sines = np.cos(angles) * factor, np.sin(angles) * factor
    table = np.stack([np.concatenate([cosine, -sines], 1), np.concatenate([sines, cosine], 1)])
    table = table.reshape(2, group_count, feed_count // group_count, 2 * feed_count)
    table = table.swapaxes(0, 1).reshape(group_count, -1, 2 * feed_count)
    return table.astype(np.float32).astype(jnp.bfloat16)


def spectral_tables(up_count, frame_count, column_count):
    spectral = np.arange(up_count)
    angles = (spectral[:, None] * spectral[None, :] % up_count) * (-2.0 * math.pi / up_count)
    factor = 1.0 / math.sqrt(column_count * up_count)
    cosine, sines = np.cos(angles) * factor, np.sin(angles) * factor
    same = np.eye(frame_count)
    sample_count = frame_count * up_count

    def spread(entries):
        return np.einsum("uk,tv->tukv", entries, same).reshape(sample_count, sample_count)

    table = np.block([[spread(cosine), spread(sines)], [-spread(sines), spread(cosine)]])
    table = table.astype(np.float32)
    high = table.astype(jnp.bfloat16)
    low = (table - high.astype(np.float32)).astype(jnp.bfloat16)
    return high, low


def form_kernel(me_ref, after_ref, table_ref, gain_real_ref, gain_imag_ref, real_ref, imag_ref, *refs):
    out_refs, gains_ref = refs[:-1], refs[-1]
    channels, pols, _, beams, samples = out_refs[0].shape
    for c in range(channels):
        gains_ref[0, c * pols : (c + 1) * pols] = gain_real_ref[c, 0]
        gains_ref[1, c * pols : (c + 1) * pols] = gain_imag_ref[c, 0]
    gains_real, gains_imag = gains_ref[0].T, gains_ref[1].T
    table = jnp.concatenate([table_ref[me_ref[0] ^ r] for r in range(len(out_refs))], axis=0)
    for c in range(channels):
        columns = []
        for p in range(pols):
            j = c * pols + p
            gain_real, gain_imag = gains_real[:, j : j + 1], gains_imag[:, j : j + 1]
            real = real_ref[c, 0, p].astype(jnp.float32)
            imag = imag_ref[c, 0, p].astype(jnp.float32)
            real_part = (gain_real * real - gain_imag * imag).astype(jnp.bfloat16)
            imag_part = (gain_real * imag + gain_imag * real).astype(jnp.bfloat16)
            columns.append(jnp.concatenate([real_part, imag_part], axis=0))
        calibrated = jnp.concatenate(columns, axis=1)
        formed = jnp.dot(table, calibrated, preferred_element_type=jnp.float32)
        formed = formed.astype(jnp.bfloat16)
        for p in range(pols):
            for r, out_ref in enumerate(out_refs):
                for a in range(2):
                    row = (r * 2 + a) * beams
                    out_ref[c, p, a] = formed[row : row + beams, p * samples : (p + 1) * samples]


def detect_kernel(me_ref, after_ref, before_ref, high_ref, low_ref, order_ref, *refs):
    formed_refs, (out_ref, sum_ref, rows_ref) = refs[:-3], refs[-3:]
    owners, channels, own, _ = out_ref.shape
    columns = len(formed_refs)
    _, pols, _, beams, samples = formed_refs[0].shape
    for c in range(channels):
        for r, formed_ref in enumerate(formed_refs):
            y = me_ref[0] ^ r
            for p in range(pols):
                for a in range(2):
                    rows_ref[p, y, :, a * samples : (a + 1) * samples] = formed_ref[c, p, a]
        rows = rows_ref[...].reshape(pols * columns * beams, 2 * samples)
        spectra = jnp.dot(rows, high_ref[...], preferred_element_type=jnp.float32) + jnp.dot(
            rows, low_ref[...], preferred_element_type=jnp.float32
        )
        real, imag = [], []
        for p in range(pols):
            g = [spectra[(p * columns + y) * beams :][:beams] for y in range(columns)]
            even_sum, even_diff = g[0] + g[2], g[0] - g[2]
            odd_sum, odd_diff = g[1] + g[3], g[1] - g[3]
            zero, two = even_sum + odd_sum, even_sum - odd_sum
            dr, di = even_diff[:, :samples], even_diff[:, samples:]
            qr, qi = odd_diff[:, :samples], odd_diff[:, samples:]
            real.append([zero[:, :samples], dr + qi, two[:, :samples], dr - qi])
            imag.append([zero[:, samples:], di - qr, two[:, samples:], di + qr])
        stokes, total = [], None
        for e in range(columns):
            xr, xi, yr, yi = real[0][e], imag[0][e], real[1][e], imag[1][e]
            intensity = (xr * xr + xi * xi + yr * yr + yi * yi).astype(jnp.bfloat16)
            circular = (2.0 * (xi * yr - xr * yi)).astype(jnp.bfloat16)
            stokes.append(jnp.concatenate([intensity, circular], axis=1))
            part = intensity.astype(jnp.float32)
            total = part if total is None else total + part
        sum_ref[0, c : c + 1, :] = jnp.sum(total, axis=0, keepdims=True)
        ordered = jnp.dot(
            order_ref[...], jnp.concatenate(stokes, axis=0), preferred_element_type=jnp.float32
        )
        for d in range(owners):
            out_ref[d, c] = ordered[d * own : (d + 1) * own].astype(jnp.bfloat16)


def flag_kernel(group_ref, common_ref, mask_ref, *refs):
    chunk_refs, out_ref, power_ref = refs[:-2], refs[-2], refs[-1]
    sources, _, beams, width = chunk_refs[0].shape
    samples = width // 2
    sizes = [chunk_ref.shape[1] for chunk_ref in chunk_refs]
    local = sum(sizes)

    def measure(s, level):
        first = s * local
        for size, chunk_ref in zip(sizes, chunk_refs):
            common = common_ref[pl.ds(first, size)]
            cleaned = chunk_ref[s, :, :, :samples].astype(jnp.float32) - common
            squares = (cleaned * cleaned).reshape(size * beams, samples)
            high = squares.astype(jnp.bfloat16)
            low = (squares - high.astype(jnp.float32)).astype(jnp.bfloat16)
            squares = jnp.concatenate([high, low], axis=1)
            power = jnp.dot(squares, group_ref[...], preferred_element_type=jnp.float32)
            power = power.reshape(size, beams, samples)
            power_ref[pl.ds(first, size)] = power
            level = level + jnp.sum(power, axis=0)
            first = first + size
        return level

    level = lax.fori_loop(0, sources, measure, jnp.zeros((beams, samples), jnp.float32))
    level = jnp.sum(level, axis=1, keepdims=True) / float(sources * local * samples) + epsilon
    scale = jnp.broadcast_to(0.5 / level, (beams, samples))

    def flag(s, carry):
        channel = s * local
        for size, chunk_ref in zip(sizes, chunk_refs):
            for c in range(size):
                row = chunk_ref[s, c].astype(jnp.float32)
                cleaned = row[:, :samples] - common_ref[channel]
                weight = mask_ref[channel] / (1.0 + power_ref[channel] * scale)
                where = pl.ds(pl.multiple_of(channel * samples, samples), samples)
                out_ref[0, :, where] = (cleaned * weight).astype(jnp.bfloat16)
                out_ref[1, :, where] = (row[:, samples:] * weight).astype(jnp.bfloat16)
                channel = channel + 1
        return carry

    lax.fori_loop(0, sources, flag, 0)


def whole_spec(array):
    return pl.BlockSpec(array.shape, lambda *_: (0,) * array.ndim)


def form(me, after, table, gains, volts, first, per_chunk, step, groups):
    real, imag = volts
    _, _, pols, feeds, samples = real.shape
    steps = per_chunk // step
    gain_spec = pl.BlockSpec((step, 1, pols, feeds), lambda i: (first // step + i, 0, 0, 0))
    volt_spec = pl.BlockSpec(
        (step, 1, pols, feeds, samples), lambda i: (first // step + i, 0, 0, 0, 0)
    )
    beams = feeds // groups
    return pl.pallas_call(
        form_kernel,
        grid=(steps,),
        in_specs=[
            pl.BlockSpec(memory_space=pltpu.SMEM),
            pl.BlockSpec(memory_space=pl.ANY),
            whole_spec(table),
            gain_spec,
            gain_spec,
            volt_spec,
            volt_spec,
        ],
        out_specs=[pl.BlockSpec((step, pols, 2, beams, samples), lambda i: (i, 0, 0, 0, 0))]
        * groups,
        out_shape=[jax.ShapeDtypeStruct((per_chunk, pols, 2, beams, samples), jnp.bfloat16)]
        * groups,
        scratch_shapes=[pltpu.VMEM((2, 8, feeds), jnp.float32)],
        cost_estimate=pl.CostEstimate(
            flops=1000,
            bytes_accessed=1000,
            transcendentals=0,
        ),
        compiler_params=pltpu.CompilerParams(vmem_limit_bytes=60 << 20),
        name="form",
    )(me, after, table, *gains, real, imag)


def detect(me, tables, order, formed, after, step, owners):
    columns = len(formed)
    per_chunk, pols, _, beams, samples = formed[0].shape
    steps = per_chunk // step
    own = columns * beams // owners
    block_spec = pl.BlockSpec((step, pols, 2, beams, samples), lambda i: (i, 0, 0, 0, 0))
    return pl.pallas_call(
        detect_kernel,
        grid=(steps,),
        in_specs=[
            pl.BlockSpec(memory_space=pltpu.SMEM),
            pl.BlockSpec(memory_space=pl.ANY),
            pl.BlockSpec(memory_space=pl.ANY),
            *[whole_spec(table) for table in tables],
            whole_spec(order),
            *[block_spec] * columns,
        ],
        out_specs=[
            pl.BlockSpec((owners, step, own, 2 * samples), lambda i: (0, i, 0, 0)),
            pl.BlockSpec((1, step, samples), lambda i: (i, 0, 0)),
        ],
        out_shape=[
            jax.ShapeDtypeStruct((owners, per_chunk, own, 2 * samples), jnp.bfloat16),
            jax.ShapeDtypeStruct((steps, step, samples), jnp.float32),
        ],
        scratch_shapes=[pltpu.VMEM((pols, columns, beams, 2 * samples), jnp.bfloat16)],
        cost_estimate=pl.CostEstimate(
            flops=per_chunk * DETECT_FLOPS,
            bytes_accessed=1000,
            transcendentals=0,
        ),
        compiler_params=pltpu.CompilerParams(vmem_limit_bytes=60 << 20),
        name="detect",
    )(me, *after, *tables, order, *formed)


def soft_flag(owned, common, mask, frame_count):
    sources, _, own, width = owned[0].shape
    samples = width // 2
    channels = common.shape[0]
    block = 16 if own % 16 == 0 else own
    group = np.kron(np.eye(samples // frame_count), np.ones((frame_count, frame_count)))
    group = jnp.asarray(np.concatenate([group, group]) / frame_count, jnp.bfloat16)
    return pl.pallas_call(
        flag_kernel,
        grid=(own // block,),
        in_specs=[
            whole_spec(group),
            whole_spec(common),
            whole_spec(mask),
            *[
                pl.BlockSpec((sources, one.shape[1], block, width), lambda i: (0, 0, i, 0))
                for one in owned
            ],
        ],
        out_specs=pl.BlockSpec((2, block, channels * samples), lambda i: (0, i, 0)),
        out_shape=jax.ShapeDtypeStruct((2, own, channels * samples), jnp.bfloat16),
        scratch_shapes=[pltpu.VMEM((channels, block, samples), jnp.float32)],
        cost_estimate=pl.CostEstimate(
            flops=channels * own * samples * samples * 4,
            bytes_accessed=channels * own * samples * 8,
            transcendentals=0,
        ),
        compiler_params=pltpu.CompilerParams(vmem_limit_bytes=60 << 20),
        name="flag",
    )(group, common, mask, *owned)


def swap(one, axis, apart):
    return lax.ppermute(one, axis, [(i, i ^ apart) for i in range(lax.axis_size(axis))])


def body(voltage_real, voltage_imag, gain_real, gain_imag, channel_mask, beam_owner):
    local, _, pols, feeds, samples = voltage_real.shape
    frame_count = samples // UP
    owners, groups = lax.axis_size("chan"), lax.axis_size("grp")
    channels = local * owners
    unit = local // sum(SHARES)
    sizes = [share * unit for share in SHARES] if local == unit * sum(SHARES) else [1] * local
    chunks = len(sizes)
    firsts = [sum(sizes[:chunk]) for chunk in range(chunks)]
    step = math.gcd(*sizes, 2)

    gains = (gain_real, gain_imag)
    mine = lax.axis_index("grp")
    table = jnp.asarray(beam_table(feeds, groups))
    me = mine.astype(jnp.int32).reshape(1)
    tables = [jnp.asarray(one) for one in spectral_tables(UP, frame_count, groups)]
    slots = beam_owner.shape[1]
    order = (beam_owner[0][:, None] == jnp.arange(slots, dtype=jnp.int32)[None, :]).astype(
        jnp.bfloat16
    )
    mask = jnp.repeat(channel_mask.astype(jnp.float32), frame_count).reshape(channels, 1, samples)
    volts = (voltage_real, voltage_imag)
    turned, owned, sums = [], [], []
    after = me
    for chunk in range(chunks + 1):
        if chunk < chunks:
            formed = form(
                me, after, table, gains, volts, firsts[chunk], sizes[chunk], step, groups
            )
            turned.append([swap(one, "grp", r) if r else one for r, one in enumerate(formed)])
            after = formed[0]
        if chunk > 0:
            before = owned[-2:-1] or [me]
            stokes, part = detect(
                me, tables, order, turned[chunk - 1], [after, before[0]], step, owners
            )
            owned.append(lax.all_to_all(stokes, "chan", split_axis=0, concat_axis=0, tiled=True))
            sums.append(part.reshape(sizes[chunk - 1], samples))
            after = stokes
    common = jnp.concatenate(sums, axis=0)
    for bit in range(groups.bit_length() - 1):
        common = common + swap(common, "grp", 1 << bit)
    common = common / float(feeds * groups)
    piece = local // groups
    common_piece = lax.dynamic_slice_in_dim(common, mine * piece, piece).reshape(-1)
    near = lax.axis_index("chan")
    others = [swap(common, "chan", r) if r else common for r in range(owners)]
    common = jnp.zeros((owners, local, samples), jnp.float32)
    for r, other in enumerate(others):
        common = lax.dynamic_update_index_in_dim(common, other, near ^ r, 0)
    flagged = soft_flag(owned, common.reshape(channels, 1, samples), mask, frame_count)
    return (flagged, common_piece)


def solution(mesh):
    in_specs = (
        P("chan", "grp", None, None, None),
        P("chan", "grp", None, None, None),
        P("chan", "grp", None, None),
        P("chan", "grp", None, None),
        P(),
        P("grp", None),
    )
    out_specs = (P(None, ("chan", "grp"), None), P(("chan", "grp")))
    return jax.shard_map(body, mesh=mesh, in_specs=in_specs, out_specs=out_specs, check_vma=False)
```

```python
import functools
import math

import jax
import jax.numpy as jnp
import numpy as np
from jax import lax
from jax.experimental import pallas as pl
from jax.experimental.pallas import tpu as pltpu
from jax.sharding import PartitionSpec as P

UP = 16
QUAD = 4
SHARES = (2, 4, 5, 6, 6, 5, 4)
BEHIND = 2
DETECT_FLOPS = 3_000_000_000

epsilon = 1e-05


def beam_table(feed_count, group_count):
    counter = np.arange(feed_count)
    angles = (counter[:, None] * counter[None, :] % feed_count) * (-2.0 * math.pi / feed_count)
    factor = 1.0 / math.sqrt(feed_count)
    cosine, sines = np.cos(angles) * factor, np.sin(angles) * factor
    table = np.stack([np.concatenate([cosine, -sines], 1), np.concatenate([sines, cosine], 1)])
    table = table.reshape(2, group_count, feed_count // group_count, 2 * feed_count)
    table = table.swapaxes(0, 1).reshape(group_count, -1, 2 * feed_count)
    return table.astype(np.float32).astype(jnp.bfloat16)


def spectral_tables(up_count, frame_count, column_count):
    spectral = np.arange(up_count)
    angles = (spectral[:, None] * spectral[None, :] % up_count) * (-2.0 * math.pi / up_count)
    factor = 1.0 / math.sqrt(column_count * up_count)
    cosine, sines = np.cos(angles) * factor, np.sin(angles) * factor
    same = np.eye(frame_count)
    sample_count = frame_count * up_count

    def spread(entries):
        return np.einsum("uk,tv->tukv", entries, same).reshape(sample_count, sample_count)

    table = np.block([[spread(cosine), spread(sines)], [-spread(sines), spread(cosine)]])
    table = table.astype(np.float32)
    high = table.astype(jnp.bfloat16)
    low = (table - high.astype(np.float32)).astype(jnp.bfloat16)
    return high, low


def form_kernel(me_ref, after_ref, table_ref, gain_real_ref, gain_imag_ref, real_ref, imag_ref, *refs):
    out_refs, gains_ref = refs[:-1], refs[-1]
    channels, pols, _, beams, samples = out_refs[0].shape
    for c in range(channels):
        gains_ref[0, c * pols : (c + 1) * pols] = gain_real_ref[c, 0]
        gains_ref[1, c * pols : (c + 1) * pols] = gain_imag_ref[c, 0]
    gains_real, gains_imag = gains_ref[0].T, gains_ref[1].T
    table = jnp.concatenate([table_ref[me_ref[0] ^ r] for r in range(len(out_refs))], axis=0)
    for c in range(channels):
        columns = []
        for p in range(pols):
            j = c * pols + p
            gain_real, gain_imag = gains_real[:, j : j + 1], gains_imag[:, j : j + 1]
            real = real_ref[c, 0, p].astype(jnp.float32)
            imag = imag_ref[c, 0, p].astype(jnp.float32)
            real_part = (gain_real * real - gain_imag * imag).astype(jnp.bfloat16)
            imag_part = (gain_real * imag + gain_imag * real).astype(jnp.bfloat16)
            columns.append(jnp.concatenate([real_part, imag_part], axis=0))
        calibrated = jnp.concatenate(columns, axis=1)
        formed = jnp.dot(table, calibrated, preferred_element_type=jnp.float32)
        formed = formed.astype(jnp.bfloat16)
        for p in range(pols):
            for r, out_ref in enumerate(out_refs):
                for a in range(2):
                    row = (r * 2 + a) * beams
                    out_ref[c, p, a] = formed[row : row + beams, p * samples : (p + 1) * samples]


def detect_kernel(rows_count, me_ref, *refs):
    high_ref, low_ref, order_ref, *refs = refs[2:]
    columns = rows_count
    formed_refs, out_refs, (sum_ref, rows_ref) = refs[:columns], refs[columns:-2], refs[-2:]
    quad, channels, own, _ = out_refs[0].shape
    _, pols, _, beams, samples = formed_refs[0].shape
    for c in range(channels):
        for r, formed_ref in enumerate(formed_refs):
            y = me_ref[0] ^ r
            for p in range(pols):
                for a in range(2):
                    rows_ref[p, y, :, a * samples : (a + 1) * samples] = formed_ref[c, p, a]
        rows = rows_ref[...].reshape(pols * columns * beams, 2 * samples)
        spectra = jnp.dot(rows, high_ref[...], preferred_element_type=jnp.float32) + jnp.dot(
            rows, low_ref[...], preferred_element_type=jnp.float32
        )
        real, imag = [], []
        for p in range(pols):
            g = [spectra[(p * columns + y) * beams :][:beams] for y in range(columns)]
            even_sum, even_diff = g[0] + g[2], g[0] - g[2]
            odd_sum, odd_diff = g[1] + g[3], g[1] - g[3]
            zero, two = even_sum + odd_sum, even_sum - odd_sum
            dr, di = even_diff[:, :samples], even_diff[:, samples:]
            qr, qi = odd_diff[:, :samples], odd_diff[:, samples:]
            real.append([zero[:, :samples], dr + qi, two[:, :samples], dr - qi])
            imag.append([zero[:, samples:], di - qr, two[:, samples:], di + qr])
        stokes, total = [], None
        for e in range(columns):
            xr, xi, yr, yi = real[0][e], imag[0][e], real[1][e], imag[1][e]
            intensity = (xr * xr + xi * xi + yr * yr + yi * yi).astype(jnp.bfloat16)
            circular = (2.0 * (xi * yr - xr * yi)).astype(jnp.bfloat16)
            stokes.append(jnp.concatenate([intensity, circular], axis=1))
            part = intensity.astype(jnp.float32)
            total = part if total is None else total + part
        sum_ref[0, c : c + 1, :] = jnp.sum(total, axis=0, keepdims=True)
        ordered = jnp.dot(
            order_ref[...], jnp.concatenate(stokes, axis=0), preferred_element_type=jnp.float32
        )
        ordered = ordered.astype(jnp.bfloat16)
        for r in range(ordered.shape[0] // own):
            block = ordered[r * own : (r + 1) * own]
            out_refs[r // quad][r % quad, c] = block


def flag_kernel(layout, me_ref, group_ref, common_ref, mask_ref, *refs):
    block_refs, out_ref, power_ref = refs[:-2], refs[-2], refs[-1]
    beams, width = block_refs[0].shape[3:]
    samples = width // 2
    local = layout[-1][0] + layout[-1][1]
    channels = common_ref.shape[0]
    near = me_ref[1]

    def blocks(work, carry):
        for (first, size), block_ref in zip(layout, block_refs):
            fours = block_ref.shape[1]

            def step(j, carry):
                q, i = j // fours, j % fours
                source = (near // QUAD * QUAD ^ i * QUAD) + q
                return work(carry, block_ref.at[q, i], source * local + first, size)

            carry = lax.fori_loop(0, QUAD * fours, step, carry)
        return carry

    def measure(level, block_ref, channel, size):
        common = common_ref[pl.ds(channel, size)]
        cleaned = block_ref[:, :, :samples].astype(jnp.float32) - common
        squares = (cleaned * cleaned).reshape(size * beams, samples)
        high = squares.astype(jnp.bfloat16)
        low = (squares - high.astype(jnp.float32)).astype(jnp.bfloat16)
        squares = jnp.concatenate([high, low], axis=1)
        power = jnp.dot(squares, group_ref[...], preferred_element_type=jnp.float32)
        power = power.reshape(size, beams, samples)
        power_ref[pl.ds(channel, size)] = power
        return level + jnp.sum(power, axis=0)

    level = blocks(measure, jnp.zeros((beams, samples), jnp.float32))
    level = jnp.sum(level, axis=1, keepdims=True) / float(channels * samples) + epsilon
    scale = jnp.broadcast_to(0.5 / level, (beams, samples))

    def flag(carry, block_ref, channel, size):
        for c in range(size):
            row = block_ref[c].astype(jnp.float32)
            cleaned = row[:, :samples] - common_ref[channel + c]
            weight = mask_ref[channel + c] / (1.0 + power_ref[channel + c] * scale)
            where = pl.ds(pl.multiple_of((channel + c) * samples, samples), samples)
            out_ref[0, :, where] = (cleaned * weight).astype(jnp.bfloat16)
            out_ref[1, :, where] = (row[:, samples:] * weight).astype(jnp.bfloat16)
        return carry

    blocks(flag, 0)


def whole_spec(array):
    return pl.BlockSpec(array.shape, lambda *_: (0,) * array.ndim)


def form(me, after, table, gains, volts, first, per_chunk, step, groups):
    real, imag = volts
    _, _, pols, feeds, samples = real.shape
    steps = per_chunk // step
    gain_spec = pl.BlockSpec((step, 1, pols, feeds), lambda i: (first // step + i, 0, 0, 0))
    volt_spec = pl.BlockSpec(
        (step, 1, pols, feeds, samples), lambda i: (first // step + i, 0, 0, 0, 0)
    )
    beams = feeds // groups
    return pl.pallas_call(
        form_kernel,
        grid=(steps,),
        in_specs=[
            pl.BlockSpec(memory_space=pltpu.SMEM),
            pl.BlockSpec(memory_space=pl.ANY),
            whole_spec(table),
            gain_spec,
            gain_spec,
            volt_spec,
            volt_spec,
        ],
        out_specs=[pl.BlockSpec((step, pols, 2, beams, samples), lambda i: (i, 0, 0, 0, 0))]
        * groups,
        out_shape=[jax.ShapeDtypeStruct((per_chunk, pols, 2, beams, samples), jnp.bfloat16)]
        * groups,
        scratch_shapes=[pltpu.VMEM((2, 8, feeds), jnp.float32)],
        cost_estimate=pl.CostEstimate(
            flops=1000,
            bytes_accessed=1000,
            transcendentals=0,
        ),
        compiler_params=pltpu.CompilerParams(vmem_limit_bytes=60 << 20),
        name="form",
    )(me, after, table, *gains, real, imag)


def detect(me, tables, order, formed, after, step, owners):
    columns = len(formed)
    per_chunk, pols, _, beams, samples = formed[0].shape
    steps = per_chunk // step
    own = columns * beams // owners
    counts = [QUAD] * (owners // QUAD)
    block_spec = pl.BlockSpec((step, pols, 2, beams, samples), lambda i: (i, 0, 0, 0, 0))
    return pl.pallas_call(
        functools.partial(detect_kernel, columns),
        grid=(steps,),
        in_specs=[
            pl.BlockSpec(memory_space=pltpu.SMEM),
            *[pl.BlockSpec(memory_space=pl.ANY)] * len(after),
            *[whole_spec(table) for table in tables],
            whole_spec(order),
            *[block_spec] * columns,
        ],
        out_specs=[
            *[
                pl.BlockSpec((count, step, own, 2 * samples), lambda i: (0, i, 0, 0))
                for count in counts
            ],
            pl.BlockSpec((1, step, samples), lambda i: (i, 0, 0)),
        ],
        out_shape=[
            *[
                jax.ShapeDtypeStruct((count, per_chunk, own, 2 * samples), jnp.bfloat16)
                for count in counts
            ],
            jax.ShapeDtypeStruct((steps, step, samples), jnp.float32),
        ],
        scratch_shapes=[pltpu.VMEM((pols, columns, beams, 2 * samples), jnp.bfloat16)],
        cost_estimate=pl.CostEstimate(
            flops=per_chunk * DETECT_FLOPS,
            bytes_accessed=1000,
            transcendentals=0,
        ),
        compiler_params=pltpu.CompilerParams(vmem_limit_bytes=60 << 20),
        name="detect",
    )(me, *after, *tables, order, *formed)


def soft_flag(me, owned, common, mask, frame_count):
    own, width = owned[0].shape[3:]
    sizes = [one.shape[2] for one in owned]
    layout = [(sum(sizes[:i]), size) for i, size in enumerate(sizes)]
    samples = width // 2
    channels = common.shape[0]
    rows = 16 if own % 16 == 0 else own
    group = np.kron(np.eye(samples // frame_count), np.ones((frame_count, frame_count)))
    group = jnp.asarray(np.concatenate([group, group]) / frame_count, jnp.bfloat16)
    return pl.pallas_call(
        functools.partial(flag_kernel, layout),
        grid=(own // rows,),
        in_specs=[
            pl.BlockSpec(memory_space=pltpu.SMEM),
            whole_spec(group),
            whole_spec(common),
            whole_spec(mask),
            *[
                pl.BlockSpec((*one.shape[:3], rows, width), lambda i: (0, 0, 0, i, 0))
                for one in owned
            ],
        ],
        out_specs=pl.BlockSpec((2, rows, channels * samples), lambda i: (0, i, 0)),
        out_shape=jax.ShapeDtypeStruct((2, own, channels * samples), jnp.bfloat16),
        scratch_shapes=[pltpu.VMEM((channels, rows, samples), jnp.float32)],
        cost_estimate=pl.CostEstimate(
            flops=channels * own * samples * samples * 4,
            bytes_accessed=channels * own * samples * 8,
            transcendentals=0,
        ),
        compiler_params=pltpu.CompilerParams(vmem_limit_bytes=60 << 20),
        name="flag",
    )(me, group, common, mask, *owned)


def swap(one, axis, apart):
    return lax.ppermute(one, axis, [(i, i ^ apart) for i in range(lax.axis_size(axis))])


def body(voltage_real, voltage_imag, gain_real, gain_imag, channel_mask, beam_owner):
    local, _, pols, feeds, samples = voltage_real.shape
    frame_count = samples // UP
    owners, groups = lax.axis_size("chan"), lax.axis_size("grp")
    channels = local * owners
    unit = local // sum(SHARES)
    sizes = [share * unit for share in SHARES] if local == unit * sum(SHARES) else [1] * local
    chunks = len(sizes)
    firsts = [sum(sizes[:chunk]) for chunk in range(chunks)]
    step = math.gcd(*sizes, 2)

    gains = (gain_real, gain_imag)
    mine = lax.axis_index("grp")
    table = jnp.asarray(beam_table(feeds, groups))
    near = lax.axis_index("chan")
    me = jnp.stack([mine, near]).astype(jnp.int32)
    fours = [list(range(i, i + QUAD)) for i in range(0, owners, QUAD)]
    tables = [jnp.asarray(one) for one in spectral_tables(UP, frame_count, groups)]
    slots = beam_owner.shape[1]
    wanted = beam_owner[0].reshape(owners, slots // owners)
    first_four = near // QUAD * QUAD
    wanted = wanted[first_four ^ jnp.arange(owners, dtype=jnp.int32)].reshape(slots)
    order = (wanted[:, None] == jnp.arange(slots, dtype=jnp.int32)[None, :]).astype(jnp.bfloat16)
    mask = jnp.repeat(channel_mask.astype(jnp.float32), frame_count).reshape(channels, 1, samples)
    volts = (voltage_real, voltage_imag)
    turned, owned, sums = [], [], []
    after = me
    for chunk in range(chunks + 2):
        if chunk < chunks:
            formed = form(
                me, after, table, gains, volts, firsts[chunk], sizes[chunk], step, groups
            )
            turned.append([swap(one, "grp", r) if r else one for r, one in enumerate(formed)])
            after = formed[0]
        if 0 < chunk <= chunks:
            before = owned[-BEHIND] if len(owned) >= BEHIND else me
            *quads, part = detect(
                me, tables, order, turned[chunk - 1], [after, before], step, owners
            )
            quads = [swap(one, "chan", QUAD * i) if i else one for i, one in enumerate(quads)]
            after = part
        if chunk > 1:
            if chunk <= chunks:
                waiting, part = lax.optimization_barrier((waiting, part))
            owned.append(
                lax.all_to_all(
                    jnp.stack(waiting, axis=1),
                    "chan",
                    split_axis=0,
                    concat_axis=0,
                    axis_index_groups=fours,
                    tiled=True,
                )
            )
        if 0 < chunk <= chunks:
            waiting = quads
            sums.append(part.reshape(sizes[chunk - 1], samples))
    common = jnp.concatenate(sums, axis=0).reshape(groups, local // groups, samples)
    mine_of = [common[mine ^ r] for r in range(groups)]
    common = mine_of[0]
    for r in range(1, groups):
        common = common + swap(mine_of[r], "grp", r)
    common = common / float(feeds * groups)
    common_piece = common.reshape(-1)
    shared = common[None]
    for bit in range(owners.bit_length() - 1):
        other = swap(shared, "chan", 1 << bit)
        low = (near >> bit) % 2 == 0
        shared = jnp.where(low, jnp.stack([shared, other]), jnp.stack([other, shared]))
        shared = shared.reshape(-1, local // groups, samples)
    common = jnp.zeros((owners, groups, local // groups, samples), jnp.float32)
    for r in range(groups):
        other = swap(shared, "grp", r) if r else shared
        common = lax.dynamic_update_index_in_dim(common, other, mine ^ r, 1)
    flagged = soft_flag(me, owned, common.reshape(channels, 1, samples), mask, frame_count)
    return (flagged, common_piece)


def solution(mesh):
    in_specs = (
        P("chan", "grp", None, None, None),
        P("chan", "grp", None, None, None),
        P("chan", "grp", None, None),
        P("chan", "grp", None, None),
        P(),
        P("grp", None),
    )
    out_specs = (P(None, ("chan", "grp"), None), P(("chan", "grp")))
    return jax.shard_map(body, mesh=mesh, in_specs=in_specs, out_specs=out_specs, check_vma=False)
```

```python
import functools
import math

import jax
import jax.numpy as jnp
import numpy as np
from jax import lax
from jax.experimental import pallas as pl
from jax.experimental.pallas import tpu as pltpu
from jax.sharding import PartitionSpec as P

UP = 16
SHARES = (2, 4, 5, 6, 7, 8)
DIRECT = (False,) * 6
DETECT_FLOPS = 1_600_000_000

epsilon = 1e-05


def beam_table(feed_count, group_count):
    counter = np.arange(feed_count)
    angles = (counter[:, None] * counter[None, :] % feed_count) * (-2.0 * math.pi / feed_count)
    factor = 1.0 / math.sqrt(feed_count)
    cosine, sines = np.cos(angles) * factor, np.sin(angles) * factor
    table = np.stack([np.concatenate([cosine, -sines], 1), np.concatenate([sines, cosine], 1)])
    table = table.reshape(2, group_count, feed_count // group_count, 2 * feed_count)
    table = table.swapaxes(0, 1).reshape(group_count, -1, 2 * feed_count)
    return table.astype(np.float32).astype(jnp.bfloat16)


def spectral_tables(up_count, frame_count, column_count):
    spectral = np.arange(up_count)
    angles = (spectral[:, None] * spectral[None, :] % up_count) * (-2.0 * math.pi / up_count)
    factor = 1.0 / math.sqrt(column_count * up_count)
    cosine, sines = np.cos(angles) * factor, np.sin(angles) * factor
    same = np.eye(frame_count)
    sample_count = frame_count * up_count

    def spread(entries):
        return np.einsum("uk,tv->tukv", entries, same).reshape(sample_count, sample_count)

    table = np.block([[spread(cosine), spread(sines)], [-spread(sines), spread(cosine)]])
    table = table.astype(np.float32)
    high = table.astype(jnp.bfloat16)
    low = (table - high.astype(np.float32)).astype(jnp.bfloat16)
    return high, low


def form_kernel(me_ref, after_ref, table_ref, gain_real_ref, gain_imag_ref, real_ref, imag_ref, *refs):
    out_refs, gains_ref = refs[:-1], refs[-1]
    channels, pols, _, beams, samples = out_refs[0].shape
    for c in range(channels):
        gains_ref[0, c * pols : (c + 1) * pols] = gain_real_ref[c, 0]
        gains_ref[1, c * pols : (c + 1) * pols] = gain_imag_ref[c, 0]
    gains_real, gains_imag = gains_ref[0].T, gains_ref[1].T
    table = jnp.concatenate([table_ref[me_ref[0] ^ r] for r in range(len(out_refs))], axis=0)
    for c in range(channels):
        columns = []
        for p in range(pols):
            j = c * pols + p
            gain_real, gain_imag = gains_real[:, j : j + 1], gains_imag[:, j : j + 1]
            real = real_ref[c, 0, p].astype(jnp.float32)
            imag = imag_ref[c, 0, p].astype(jnp.float32)
            real_part = (gain_real * real - gain_imag * imag).astype(jnp.bfloat16)
            imag_part = (gain_real * imag + gain_imag * real).astype(jnp.bfloat16)
            columns.append(jnp.concatenate([real_part, imag_part], axis=0))
        calibrated = jnp.concatenate(columns, axis=1)
        formed = jnp.dot(table, calibrated, preferred_element_type=jnp.float32)
        formed = formed.astype(jnp.bfloat16)
        for p in range(pols):
            for r, out_ref in enumerate(out_refs):
                for a in range(2):
                    row = (r * 2 + a) * beams
                    out_ref[c, p, a] = formed[row : row + beams, p * samples : (p + 1) * samples]


def detect_kernel(columns, me_ref, after_ref, before_ref, high_ref, low_ref, order_ref, *refs):
    formed_refs, out_refs, (sum_ref, rows_ref) = refs[:columns], refs[columns:-2], refs[-2:]
    owners, channels, own, _ = out_refs[0].shape
    _, pols, _, beams, samples = formed_refs[0].shape
    for c in range(channels):
        for r, formed_ref in enumerate(formed_refs):
            y = me_ref[0] ^ r
            for p in range(pols):
                for a in range(2):
                    rows_ref[p, y, :, a * samples : (a + 1) * samples] = formed_ref[c, p, a]
        rows = rows_ref[...].reshape(pols * columns * beams, 2 * samples)
        spectra = jnp.dot(rows, high_ref[...], preferred_element_type=jnp.float32) + jnp.dot(
            rows, low_ref[...], preferred_element_type=jnp.float32
        )
        real, imag = [], []
        for p in range(pols):
            g = [spectra[(p * columns + y) * beams :][:beams] for y in range(columns)]
            even_sum, even_diff = g[0] + g[2], g[0] - g[2]
            odd_sum, odd_diff = g[1] + g[3], g[1] - g[3]
            zero, two = even_sum + odd_sum, even_sum - odd_sum
            dr, di = even_diff[:, :samples], even_diff[:, samples:]
            qr, qi = odd_diff[:, :samples], odd_diff[:, samples:]
            real.append([zero[:, :samples], dr + qi, two[:, :samples], dr - qi])
            imag.append([zero[:, samples:], di - qr, two[:, samples:], di + qr])
        stokes, total = [], None
        for e in range(columns):
            xr, xi, yr, yi = real[0][e], imag[0][e], real[1][e], imag[1][e]
            intensity = (xr * xr + xi * xi + yr * yr + yi * yi).astype(jnp.bfloat16)
            circular = (2.0 * (xi * yr - xr * yi)).astype(jnp.bfloat16)
            stokes.append(jnp.concatenate([intensity, circular], axis=1))
            part = intensity.astype(jnp.float32)
            total = part if total is None else total + part
        sum_ref[0, c : c + 1, :] = jnp.sum(total, axis=0, keepdims=True)
        ordered = jnp.dot(
            order_ref[...], jnp.concatenate(stokes, axis=0), preferred_element_type=jnp.float32
        )
        for d in range(owners * len(out_refs)):
            block = ordered[d * own : (d + 1) * own].astype(jnp.bfloat16)
            out_refs[d // owners][d % owners, c] = block


def flag_kernel(layout, me_ref, group_ref, common_ref, mask_ref, *refs):
    chunk_refs, out_ref, power_ref = refs[:-2], refs[-2], refs[-1]
    beams, width = chunk_refs[0].shape[2:]
    samples = width // 2
    channels = common_ref.shape[0]
    local = layout[-1][0] + layout[-1][1]
    sources = channels // local

    def blocks(work, carry):
        refs = iter(chunk_refs)
        whole, single = [], []
        for first, size, count in layout:
            if count == 1:
                whole.append((first, size, next(refs)))
            else:
                single.extend((first, size, r, next(refs)) for r in range(count))

        def step(s, carry):
            for first, size, ref in whole:
                carry = work(carry, ref.at[s], s * local + first, size)
            return carry

        carry = lax.fori_loop(0, sources, step, carry)
        for first, size, r, ref in single:
            carry = work(carry, ref.at[0], (me_ref[1] ^ r) * local + first, size)
        return carry

    def measure(level, block_ref, channel, size):
        common = common_ref[pl.ds(channel, size)]
        cleaned = block_ref[:, :, :samples].astype(jnp.float32) - common
        squares = (cleaned * cleaned).reshape(size * beams, samples)
        high = squares.astype(jnp.bfloat16)
        low = (squares - high.astype(jnp.float32)).astype(jnp.bfloat16)
        squares = jnp.concatenate([high, low], axis=1)
        power = jnp.dot(squares, group_ref[...], preferred_element_type=jnp.float32)
        power = power.reshape(size, beams, samples)
        power_ref[pl.ds(channel, size)] = power
        return level + jnp.sum(power, axis=0)

    level = blocks(measure, jnp.zeros((beams, samples), jnp.float32))
    level = jnp.sum(level, axis=1, keepdims=True) / float(channels * samples) + epsilon
    scale = jnp.broadcast_to(0.5 / level, (beams, samples))

    def flag(carry, block_ref, channel, size):
        for c in range(size):
            row = block_ref[c].astype(jnp.float32)
            cleaned = row[:, :samples] - common_ref[channel + c]
            weight = mask_ref[channel + c] / (1.0 + power_ref[channel + c] * scale)
            where = pl.ds(pl.multiple_of((channel + c) * samples, samples), samples)
            out_ref[0, :, where] = (cleaned * weight).astype(jnp.bfloat16)
            out_ref[1, :, where] = (row[:, samples:] * weight).astype(jnp.bfloat16)
        return carry

    blocks(flag, 0)


def whole_spec(array):
    return pl.BlockSpec(array.shape, lambda *_: (0,) * array.ndim)


def form(me, after, table, gains, volts, first, per_chunk, step, groups):
    real, imag = volts
    _, _, pols, feeds, samples = real.shape
    steps = per_chunk // step
    gain_spec = pl.BlockSpec((step, 1, pols, feeds), lambda i: (first // step + i, 0, 0, 0))
    volt_spec = pl.BlockSpec(
        (step, 1, pols, feeds, samples), lambda i: (first // step + i, 0, 0, 0, 0)
    )
    beams = feeds // groups
    return pl.pallas_call(
        form_kernel,
        grid=(steps,),
        in_specs=[
            pl.BlockSpec(memory_space=pltpu.SMEM),
            pl.BlockSpec(memory_space=pl.ANY),
            whole_spec(table),
            gain_spec,
            gain_spec,
            volt_spec,
            volt_spec,
        ],
        out_specs=[pl.BlockSpec((step, pols, 2, beams, samples), lambda i: (i, 0, 0, 0, 0))]
        * groups,
        out_shape=[jax.ShapeDtypeStruct((per_chunk, pols, 2, beams, samples), jnp.bfloat16)]
        * groups,
        scratch_shapes=[pltpu.VMEM((2, 8, feeds), jnp.float32)],
        cost_estimate=pl.CostEstimate(
            flops=1000,
            bytes_accessed=1000,
            transcendentals=0,
        ),
        compiler_params=pltpu.CompilerParams(vmem_limit_bytes=60 << 20),
        name="form",
    )(me, after, table, *gains, real, imag)


def detect(me, tables, order, formed, after, step, owners, direct):
    columns = len(formed)
    per_chunk, pols, _, beams, samples = formed[0].shape
    steps = per_chunk // step
    own = columns * beams // owners
    counts = [1] * owners if direct else [owners]
    block_spec = pl.BlockSpec((step, pols, 2, beams, samples), lambda i: (i, 0, 0, 0, 0))
    return pl.pallas_call(
        functools.partial(detect_kernel, columns),
        grid=(steps,),
        in_specs=[
            pl.BlockSpec(memory_space=pltpu.SMEM),
            pl.BlockSpec(memory_space=pl.ANY),
            pl.BlockSpec(memory_space=pl.ANY),
            *[whole_spec(table) for table in tables],
            whole_spec(order),
            *[block_spec] * columns,
        ],
        out_specs=[
            *[
                pl.BlockSpec((count, step, own, 2 * samples), lambda i: (0, i, 0, 0))
                for count in counts
            ],
            pl.BlockSpec((1, step, samples), lambda i: (i, 0, 0)),
        ],
        out_shape=[
            *[
                jax.ShapeDtypeStruct((count, per_chunk, own, 2 * samples), jnp.bfloat16)
                for count in counts
            ],
            jax.ShapeDtypeStruct((steps, step, samples), jnp.float32),
        ],
        scratch_shapes=[pltpu.VMEM((pols, columns, beams, 2 * samples), jnp.bfloat16)],
        cost_estimate=pl.CostEstimate(
            flops=per_chunk * DETECT_FLOPS,
            bytes_accessed=1000,
            transcendentals=0,
        ),
        compiler_params=pltpu.CompilerParams(vmem_limit_bytes=60 << 20),
        name="detect",
    )(me, *after, *tables, order, *formed)


def soft_flag(me, owned, common, mask, frame_count):
    own, width = owned[0][0].shape[2:]
    sizes = [one[0].shape[1] for one in owned]
    layout = [(sum(sizes[:i]), sizes[i], len(one)) for i, one in enumerate(owned)]
    owned = [block for one in owned for block in one]
    samples = width // 2
    channels = common.shape[0]
    block = 16 if own % 16 == 0 else own
    group = np.kron(np.eye(samples // frame_count), np.ones((frame_count, frame_count)))
    group = jnp.asarray(np.concatenate([group, group]) / frame_count, jnp.bfloat16)
    return pl.pallas_call(
        functools.partial(flag_kernel, layout),
        grid=(own // block,),
        in_specs=[
            pl.BlockSpec(memory_space=pltpu.SMEM),
            whole_spec(group),
            whole_spec(common),
            whole_spec(mask),
            *[
                pl.BlockSpec((*one.shape[:2], block, width), lambda i: (0, 0, i, 0))
                for one in owned
            ],
        ],
        out_specs=pl.BlockSpec((2, block, channels * samples), lambda i: (0, i, 0)),
        out_shape=jax.ShapeDtypeStruct((2, own, channels * samples), jnp.bfloat16),
        scratch_shapes=[pltpu.VMEM((channels, block, samples), jnp.float32)],
        cost_estimate=pl.CostEstimate(
            flops=channels * own * samples * samples * 4,
            bytes_accessed=channels * own * samples * 8,
            transcendentals=0,
        ),
        compiler_params=pltpu.CompilerParams(vmem_limit_bytes=60 << 20),
        name="flag",
    )(me, group, common, mask, *owned)


def swap(one, axis, apart):
    return lax.ppermute(one, axis, [(i, i ^ apart) for i in range(lax.axis_size(axis))])


def body(voltage_real, voltage_imag, gain_real, gain_imag, channel_mask, beam_owner):
    local, _, pols, feeds, samples = voltage_real.shape
    frame_count = samples // UP
    owners, groups = lax.axis_size("chan"), lax.axis_size("grp")
    channels = local * owners
    unit = local // sum(SHARES)
    sizes = [share * unit for share in SHARES] if local == unit * sum(SHARES) else [1] * local
    chunks = len(sizes)
    firsts = [sum(sizes[:chunk]) for chunk in range(chunks)]
    step = math.gcd(*sizes, 2)

    gains = (gain_real, gain_imag)
    mine = lax.axis_index("grp")
    table = jnp.asarray(beam_table(feeds, groups))
    near = lax.axis_index("chan")
    me = jnp.stack([mine, near]).astype(jnp.int32)
    tables = [jnp.asarray(one) for one in spectral_tables(UP, frame_count, groups)]
    slots = beam_owner.shape[1]
    wanted = beam_owner[0].reshape(owners, slots // owners)
    orders = [
        (one.reshape(slots, 1) == jnp.arange(slots, dtype=jnp.int32)).astype(jnp.bfloat16)
        for one in (wanted, wanted[near ^ jnp.arange(owners, dtype=jnp.int32)])
    ]
    mask = jnp.repeat(channel_mask.astype(jnp.float32), frame_count).reshape(channels, 1, samples)
    volts = (voltage_real, voltage_imag)
    turned, owned, sums = [], [], []
    after = me
    for chunk in range(chunks + 1):
        if chunk < chunks:
            formed = form(
                me, after, table, gains, volts, firsts[chunk], sizes[chunk], step, groups
            )
            turned.append([swap(one, "grp", r) if r else one for r, one in enumerate(formed)])
            after = formed[0]
        if chunk > 0:
            direct = chunks == len(DIRECT) and DIRECT[chunk - 1]
            before = owned[-2][-1] if len(owned) > 1 else me
            *sent, part = detect(
                me,
                tables,
                orders[direct],
                turned[chunk - 1],
                [after, before],
                step,
                owners,
                direct,
            )
            if direct:
                owned.append([swap(one, "chan", r) if r else one for r, one in enumerate(sent)])
            else:
                owned.append([lax.all_to_all(*sent, "chan", split_axis=0, concat_axis=0, tiled=True)])
            sums.append(part.reshape(sizes[chunk - 1], samples))
            after = part
    common = jnp.concatenate(sums, axis=0).reshape(groups, local // groups, samples)
    mine_of = [common[mine ^ r] for r in range(groups)]
    common = mine_of[0]
    for r in range(1, groups):
        common = common + swap(mine_of[r], "grp", r)
    common = common / float(feeds * groups)
    common_piece = common.reshape(-1)
    shared = common[None]
    for bit in range(owners.bit_length() - 1):
        other = swap(shared, "chan", 1 << bit)
        low = (near >> bit) % 2 == 0
        shared = jnp.where(low, jnp.stack([shared, other]), jnp.stack([other, shared]))
        shared = shared.reshape(-1, local // groups, samples)
    common = jnp.zeros((owners, groups, local // groups, samples), jnp.float32)
    for r in range(groups):
        other = swap(shared, "grp", r) if r else shared
        common = lax.dynamic_update_index_in_dim(common, other, mine ^ r, 1)
    flagged = soft_flag(me, owned, common.reshape(channels, 1, samples), mask, frame_count)
    return (flagged, common_piece)


def solution(mesh):
    in_specs = (
        P("chan", "grp", None, None, None),
        P("chan", "grp", None, None, None),
        P("chan", "grp", None, None),
        P("chan", "grp", None, None),
        P(),
        P("grp", None),
    )
    out_specs = (P(None, ("chan", "grp"), None), P(("chan", "grp")))
    return jax.shard_map(body, mesh=mesh, in_specs=in_specs, out_specs=out_specs, check_vma=False)
```

```python
import functools
import math

import jax
import jax.numpy as jnp
import numpy as np
from jax import lax
from jax.experimental import pallas as pl
from jax.experimental.pallas import tpu as pltpu
from jax.sharding import PartitionSpec as P

UP = 16
SHARES = (2, 4, 5, 6, 7, 8)
DIRECT = (False, False, False, False, False, False)
DETECT_FLOPS = 1_600_000_000

epsilon = 1e-05


def beam_table(feed_count, group_count):
    counter = np.arange(feed_count)
    angles = (counter[:, None] * counter[None, :] % feed_count) * (-2.0 * math.pi / feed_count)
    factor = 1.0 / math.sqrt(feed_count)
    cosine, sines = np.cos(angles) * factor, np.sin(angles) * factor
    table = np.stack([np.concatenate([cosine, -sines], 1), np.concatenate([sines, cosine], 1)])
    table = table.reshape(2, group_count, feed_count // group_count, 2 * feed_count)
    table = table.swapaxes(0, 1).reshape(group_count, -1, 2 * feed_count)
    return table.astype(np.float32).astype(jnp.bfloat16)


def spectral_tables(up_count, frame_count, column_count):
    spectral = np.arange(up_count)
    angles = (spectral[:, None] * spectral[None, :] % up_count) * (-2.0 * math.pi / up_count)
    factor = 1.0 / math.sqrt(column_count * up_count)
    cosine, sines = np.cos(angles) * factor, np.sin(angles) * factor
    same = np.eye(frame_count)
    sample_count = frame_count * up_count

    def spread(entries):
        return np.einsum("uk,tv->tukv", entries, same).reshape(sample_count, sample_count)

    table = np.block([[spread(cosine), spread(sines)], [-spread(sines), spread(cosine)]])
    table = table.astype(np.float32)
    high = table.astype(jnp.bfloat16)
    low = (table - high.astype(np.float32)).astype(jnp.bfloat16)
    return high, low


def form_kernel(me_ref, after_ref, table_ref, gain_real_ref, gain_imag_ref, real_ref, imag_ref, *refs):
    out_refs, gains_ref = refs[:-1], refs[-1]
    channels, pols, _, beams, samples = out_refs[0].shape
    for c in range(channels):
        gains_ref[0, c * pols : (c + 1) * pols] = gain_real_ref[c, 0]
        gains_ref[1, c * pols : (c + 1) * pols] = gain_imag_ref[c, 0]
    gains_real, gains_imag = gains_ref[0].T, gains_ref[1].T
    table = jnp.concatenate([table_ref[me_ref[0] ^ r] for r in range(len(out_refs))], axis=0)
    for c in range(channels):
        columns = []
        for p in range(pols):
            j = c * pols + p
            gain_real, gain_imag = gains_real[:, j : j + 1], gains_imag[:, j : j + 1]
            real = real_ref[c, 0, p].astype(jnp.float32)
            imag = imag_ref[c, 0, p].astype(jnp.float32)
            real_part = (gain_real * real - gain_imag * imag).astype(jnp.bfloat16)
            imag_part = (gain_real * imag + gain_imag * real).astype(jnp.bfloat16)
            columns.append(jnp.concatenate([real_part, imag_part], axis=0))
        calibrated = jnp.concatenate(columns, axis=1)
        formed = jnp.dot(table, calibrated, preferred_element_type=jnp.float32)
        formed = formed.astype(jnp.bfloat16)
        for p in range(pols):
            for r, out_ref in enumerate(out_refs):
                for a in range(2):
                    row = (r * 2 + a) * beams
                    out_ref[c, p, a] = formed[row : row + beams, p * samples : (p + 1) * samples]


def detect_kernel(columns, ignored, me_ref, *refs):
    high_ref, low_ref, order_ref, *refs = refs[ignored:]
    formed_refs, out_refs, (sum_ref, rows_ref) = refs[:columns], refs[columns:-2], refs[-2:]
    owners, channels, own, _ = out_refs[0].shape
    _, pols, _, beams, samples = formed_refs[0].shape
    for c in range(channels):
        for r, formed_ref in enumerate(formed_refs):
            y = me_ref[0] ^ r
            for p in range(pols):
                for a in range(2):
                    rows_ref[p, y, :, a * samples : (a + 1) * samples] = formed_ref[c, p, a]
        rows = rows_ref[...].reshape(pols * columns * beams, 2 * samples)
        spectra = jnp.dot(rows, high_ref[...], preferred_element_type=jnp.float32) + jnp.dot(
            rows, low_ref[...], preferred_element_type=jnp.float32
        )
        real, imag = [], []
        for p in range(pols):
            g = [spectra[(p * columns + y) * beams :][:beams] for y in range(columns)]
            even_sum, even_diff = g[0] + g[2], g[0] - g[2]
            odd_sum, odd_diff = g[1] + g[3], g[1] - g[3]
            zero, two = even_sum + odd_sum, even_sum - odd_sum
            dr, di = even_diff[:, :samples], even_diff[:, samples:]
            qr, qi = odd_diff[:, :samples], odd_diff[:, samples:]
            real.append([zero[:, :samples], dr + qi, two[:, :samples], dr - qi])
            imag.append([zero[:, samples:], di - qr, two[:, samples:], di + qr])
        stokes, total = [], None
        for e in range(columns):
            xr, xi, yr, yi = real[0][e], imag[0][e], real[1][e], imag[1][e]
            intensity = (xr * xr + xi * xi + yr * yr + yi * yi).astype(jnp.bfloat16)
            circular = (2.0 * (xi * yr - xr * yi)).astype(jnp.bfloat16)
            stokes.append(jnp.concatenate([intensity, circular], axis=1))
            part = intensity.astype(jnp.float32)
            total = part if total is None else total + part
        sum_ref[0, c : c + 1, :] = jnp.sum(total, axis=0, keepdims=True)
        ordered = jnp.dot(
            order_ref[...], jnp.concatenate(stokes, axis=0), preferred_element_type=jnp.float32
        )
        for d in range(owners * len(out_refs)):
            block = ordered[d * own : (d + 1) * own].astype(jnp.bfloat16)
            out_refs[d // owners][d % owners, c] = block


def flag_kernel(layout, me_ref, group_ref, common_ref, mask_ref, *refs):
    chunk_refs, out_ref, power_ref = refs[:-2], refs[-2], refs[-1]
    beams, width = chunk_refs[0].shape[2:]
    samples = width // 2
    channels = common_ref.shape[0]
    local = layout[-1][0] + layout[-1][1]
    sources = channels // local

    def blocks(work, carry):
        refs = iter(chunk_refs)
        whole, single = [], []
        for first, size, count in layout:
            if count == 1:
                whole.append((first, size, next(refs)))
            else:
                single.extend((first, size, r, next(refs)) for r in range(count))

        def step(s, carry):
            for first, size, ref in whole:
                carry = work(carry, ref.at[s], s * local + first, size)
            return carry

        carry = lax.fori_loop(0, sources, step, carry)
        for first, size, r, ref in single:
            carry = work(carry, ref.at[0], (me_ref[1] ^ r) * local + first, size)
        return carry

    def measure(level, block_ref, channel, size):
        common = common_ref[pl.ds(channel, size)]
        cleaned = block_ref[:, :, :samples].astype(jnp.float32) - common
        squares = (cleaned * cleaned).reshape(size * beams, samples)
        high = squares.astype(jnp.bfloat16)
        low = (squares - high.astype(jnp.float32)).astype(jnp.bfloat16)
        squares = jnp.concatenate([high, low], axis=1)
        power = jnp.dot(squares, group_ref[...], preferred_element_type=jnp.float32)
        power = power.reshape(size, beams, samples)
        power_ref[pl.ds(channel, size)] = power
        return level + jnp.sum(power, axis=0)

    level = blocks(measure, jnp.zeros((beams, samples), jnp.float32))
    level = jnp.sum(level, axis=1, keepdims=True) / float(channels * samples) + epsilon
    scale = jnp.broadcast_to(0.5 / level, (beams, samples))

    def flag(carry, block_ref, channel, size):
        for c in range(size):
            row = block_ref[c].astype(jnp.float32)
            cleaned = row[:, :samples] - common_ref[channel + c]
            weight = mask_ref[channel + c] / (1.0 + power_ref[channel + c] * scale)
            where = pl.ds(pl.multiple_of((channel + c) * samples, samples), samples)
            out_ref[0, :, where] = (cleaned * weight).astype(jnp.bfloat16)
            out_ref[1, :, where] = (row[:, samples:] * weight).astype(jnp.bfloat16)
        return carry

    blocks(flag, 0)


def whole_spec(array):
    return pl.BlockSpec(array.shape, lambda *_: (0,) * array.ndim)


def form(me, after, table, gains, volts, first, per_chunk, step, groups):
    real, imag = volts
    _, _, pols, feeds, samples = real.shape
    steps = per_chunk // step
    gain_spec = pl.BlockSpec((step, 1, pols, feeds), lambda i: (first // step + i, 0, 0, 0))
    volt_spec = pl.BlockSpec(
        (step, 1, pols, feeds, samples), lambda i: (first // step + i, 0, 0, 0, 0)
    )
    beams = feeds // groups
    return pl.pallas_call(
        form_kernel,
        grid=(steps,),
        in_specs=[
            pl.BlockSpec(memory_space=pltpu.SMEM),
            pl.BlockSpec(memory_space=pl.ANY),
            whole_spec(table),
            gain_spec,
            gain_spec,
            volt_spec,
            volt_spec,
        ],
        out_specs=[pl.BlockSpec((step, pols, 2, beams, samples), lambda i: (i, 0, 0, 0, 0))]
        * groups,
        out_shape=[jax.ShapeDtypeStruct((per_chunk, pols, 2, beams, samples), jnp.bfloat16)]
        * groups,
        scratch_shapes=[pltpu.VMEM((2, 8, feeds), jnp.float32)],
        cost_estimate=pl.CostEstimate(
            flops=1000,
            bytes_accessed=1000,
            transcendentals=0,
        ),
        compiler_params=pltpu.CompilerParams(vmem_limit_bytes=60 << 20),
        name="form",
    )(me, after, table, *gains, real, imag)


def detect(me, tables, order, formed, after, step, owners, direct):
    columns = len(formed)
    per_chunk, pols, _, beams, samples = formed[0].shape
    steps = per_chunk // step
    own = columns * beams // owners
    counts = [1] * owners if direct else [owners]
    block_spec = pl.BlockSpec((step, pols, 2, beams, samples), lambda i: (i, 0, 0, 0, 0))
    return pl.pallas_call(
        functools.partial(detect_kernel, columns, len(after)),
        grid=(steps,),
        in_specs=[
            pl.BlockSpec(memory_space=pltpu.SMEM),
            *[pl.BlockSpec(memory_space=pl.ANY)] * len(after),
            *[whole_spec(table) for table in tables],
            whole_spec(order),
            *[block_spec] * columns,
        ],
        out_specs=[
            *[
                pl.BlockSpec((count, step, own, 2 * samples), lambda i: (0, i, 0, 0))
                for count in counts
            ],
            pl.BlockSpec((1, step, samples), lambda i: (i, 0, 0)),
        ],
        out_shape=[
            *[
                jax.ShapeDtypeStruct((count, per_chunk, own, 2 * samples), jnp.bfloat16)
                for count in counts
            ],
            jax.ShapeDtypeStruct((steps, step, samples), jnp.float32),
        ],
        scratch_shapes=[pltpu.VMEM((pols, columns, beams, 2 * samples), jnp.bfloat16)],
        cost_estimate=pl.CostEstimate(
            flops=per_chunk * DETECT_FLOPS,
            bytes_accessed=1000,
            transcendentals=0,
        ),
        compiler_params=pltpu.CompilerParams(vmem_limit_bytes=60 << 20),
        name="detect",
    )(me, *after, *tables, order, *formed)


def soft_flag(me, owned, common, mask, frame_count):
    own, width = owned[0][0].shape[2:]
    sizes = [one[0].shape[1] for one in owned]
    layout = [(sum(sizes[:i]), sizes[i], len(one)) for i, one in enumerate(owned)]
    owned = [block for one in owned for block in one]
    samples = width // 2
    channels = common.shape[0]
    block = 16 if own % 16 == 0 else own
    group = np.kron(np.eye(samples // frame_count), np.ones((frame_count, frame_count)))
    group = jnp.asarray(np.concatenate([group, group]) / frame_count, jnp.bfloat16)
    return pl.pallas_call(
        functools.partial(flag_kernel, layout),
        grid=(own // block,),
        in_specs=[
            pl.BlockSpec(memory_space=pltpu.SMEM),
            whole_spec(group),
            whole_spec(common),
            whole_spec(mask),
            *[
                pl.BlockSpec((*one.shape[:2], block, width), lambda i: (0, 0, i, 0))
                for one in owned
            ],
        ],
        out_specs=pl.BlockSpec((2, block, channels * samples), lambda i: (0, i, 0)),
        out_shape=jax.ShapeDtypeStruct((2, own, channels * samples), jnp.bfloat16),
        scratch_shapes=[pltpu.VMEM((channels, block, samples), jnp.float32)],
        cost_estimate=pl.CostEstimate(
            flops=channels * own * samples * samples * 4,
            bytes_accessed=channels * own * samples * 8,
            transcendentals=0,
        ),
        compiler_params=pltpu.CompilerParams(vmem_limit_bytes=60 << 20),
        name="flag",
    )(me, group, common, mask, *owned)


def swap(one, axis, apart):
    return lax.ppermute(one, axis, [(i, i ^ apart) for i in range(lax.axis_size(axis))])


def body(voltage_real, voltage_imag, gain_real, gain_imag, channel_mask, beam_owner):
    local, _, pols, feeds, samples = voltage_real.shape
    frame_count = samples // UP
    owners, groups = lax.axis_size("chan"), lax.axis_size("grp")
    channels = local * owners
    unit = local // sum(SHARES)
    sizes = [share * unit for share in SHARES] if local == unit * sum(SHARES) else [1] * local
    chunks = len(sizes)
    firsts = [sum(sizes[:chunk]) for chunk in range(chunks)]
    step = math.gcd(*sizes, 2)

    gains = (gain_real, gain_imag)
    mine = lax.axis_index("grp")
    table = jnp.asarray(beam_table(feeds, groups))
    near = lax.axis_index("chan")
    me = jnp.stack([mine, near]).astype(jnp.int32)
    tables = [jnp.asarray(one) for one in spectral_tables(UP, frame_count, groups)]
    slots = beam_owner.shape[1]
    wanted = beam_owner[0].reshape(owners, slots // owners)
    orders = [
        (one.reshape(slots, 1) == jnp.arange(slots, dtype=jnp.int32)).astype(jnp.bfloat16)
        for one in (wanted, wanted[near ^ jnp.arange(owners, dtype=jnp.int32)])
    ]
    mask = jnp.repeat(channel_mask.astype(jnp.float32), frame_count).reshape(channels, 1, samples)
    volts = (voltage_real, voltage_imag)
    turned, owned, sums = [], [], []
    after = me
    for chunk in range(chunks + 1):
        if chunk < chunks:
            formed = form(
                me, after, table, gains, volts, firsts[chunk], sizes[chunk], step, groups
            )
            turned.append([swap(one, "grp", r) if r else one for r, one in enumerate(formed)])
            after = formed[0]
        if chunk > 0:
            direct = chunks == len(DIRECT) and DIRECT[chunk - 1]
            before = owned[-2] if len(owned) > 1 else []
            *sent, part = detect(
                me,
                tables,
                orders[direct],
                turned[chunk - 1],
                [after, *before],
                step,
                owners,
                direct,
            )
            sums.append(part.reshape(sizes[chunk - 1], samples))
            after = part
            if chunk == chunks:
                common = jnp.concatenate(sums, axis=0).reshape(groups, local // groups, samples)
                parts = [common[mine ^ r] for r in range(groups)]
                common = parts[0]
                for r in range(1, groups):
                    common = common + swap(parts[r], "grp", r)
                common = common / float(feeds * groups)
                common_piece = common.reshape(-1)
                common, *sent = lax.optimization_barrier((common, *sent))
            if direct:
                owned.append([swap(one, "chan", r) if r else one for r, one in enumerate(sent)])
            else:
                owned.append([lax.all_to_all(*sent, "chan", split_axis=0, concat_axis=0, tiled=True)])
    shared = jnp.zeros((owners, local // groups, samples), jnp.float32)
    for r in range(owners):
        other = swap(common, "chan", r) if r else common
        shared = lax.dynamic_update_index_in_dim(shared, other, near ^ r, 0)
    common = jnp.zeros((owners, groups, local // groups, samples), jnp.float32)
    for r in range(groups):
        other = swap(shared, "grp", r) if r else shared
        common = lax.dynamic_update_index_in_dim(common, other, mine ^ r, 1)
    flagged = soft_flag(me, owned, common.reshape(channels, 1, samples), mask, frame_count)
    return (flagged, common_piece)


def solution(mesh):
    in_specs = (
        P("chan", "grp", None, None, None),
        P("chan", "grp", None, None, None),
        P("chan", "grp", None, None),
        P("chan", "grp", None, None),
        P(),
        P("grp", None),
    )
    out_specs = (P(None, ("chan", "grp"), None), P(("chan", "grp")))
    return jax.shard_map(body, mesh=mesh, in_specs=in_specs, out_specs=out_specs, check_vma=False)
```

```python
import functools
import math

import jax
import jax.numpy as jnp
import numpy as np
from jax import lax
from jax.experimental import pallas as pl
from jax.experimental.pallas import tpu as pltpu
from jax.sharding import PartitionSpec as P

UP = 16
SHARES = (2, 4, 5, 6, 7, 8)
DIRECT = (False, True, False, True, False, False)
DETECT_FLOPS = 1_600_000_000

epsilon = 1e-05


def beam_table(feed_count, group_count):
    counter = np.arange(feed_count)
    angles = (counter[:, None] * counter[None, :] % feed_count) * (-2.0 * math.pi / feed_count)
    factor = 1.0 / math.sqrt(feed_count)
    cosine, sines = np.cos(angles) * factor, np.sin(angles) * factor
    table = np.stack([np.concatenate([cosine, -sines], 1), np.concatenate([sines, cosine], 1)])
    table = table.reshape(2, group_count, feed_count // group_count, 2 * feed_count)
    table = table.swapaxes(0, 1).reshape(group_count, -1, 2 * feed_count)
    return table.astype(np.float32).astype(jnp.bfloat16)


def spectral_tables(up_count, frame_count, column_count):
    spectral = np.arange(up_count)
    angles = (spectral[:, None] * spectral[None, :] % up_count) * (-2.0 * math.pi / up_count)
    factor = 1.0 / math.sqrt(column_count * up_count)
    cosine, sines = np.cos(angles) * factor, np.sin(angles) * factor
    same = np.eye(frame_count)
    sample_count = frame_count * up_count

    def spread(entries):
        return np.einsum("uk,tv->tukv", entries, same).reshape(sample_count, sample_count)

    table = np.block([[spread(cosine), spread(sines)], [-spread(sines), spread(cosine)]])
    table = table.astype(np.float32)
    high = table.astype(jnp.bfloat16)
    low = (table - high.astype(np.float32)).astype(jnp.bfloat16)
    return high, low


def form_kernel(me_ref, after_ref, table_ref, gain_real_ref, gain_imag_ref, real_ref, imag_ref, *refs):
    out_refs, gains_ref = refs[:-1], refs[-1]
    channels, pols, _, beams, samples = out_refs[0].shape
    for c in range(channels):
        gains_ref[0, c * pols : (c + 1) * pols] = gain_real_ref[c, 0]
        gains_ref[1, c * pols : (c + 1) * pols] = gain_imag_ref[c, 0]
    gains_real, gains_imag = gains_ref[0].T, gains_ref[1].T
    table = jnp.concatenate([table_ref[me_ref[0] ^ r] for r in range(len(out_refs))], axis=0)
    for c in range(channels):
        columns = []
        for p in range(pols):
            j = c * pols + p
            gain_real, gain_imag = gains_real[:, j : j + 1], gains_imag[:, j : j + 1]
            real = real_ref[c, 0, p].astype(jnp.float32)
            imag = imag_ref[c, 0, p].astype(jnp.float32)
            real_part = (gain_real * real - gain_imag * imag).astype(jnp.bfloat16)
            imag_part = (gain_real * imag + gain_imag * real).astype(jnp.bfloat16)
            columns.append(jnp.concatenate([real_part, imag_part], axis=0))
        calibrated = jnp.concatenate(columns, axis=1)
        formed = jnp.dot(table, calibrated, preferred_element_type=jnp.float32)
        formed = formed.astype(jnp.bfloat16)
        for p in range(pols):
            for r, out_ref in enumerate(out_refs):
                for a in range(2):
                    row = (r * 2 + a) * beams
                    out_ref[c, p, a] = formed[row : row + beams, p * samples : (p + 1) * samples]


def detect_kernel(columns, ignored, me_ref, *refs):
    high_ref, low_ref, order_ref, *refs = refs[ignored:]
    formed_refs, out_refs, (sum_ref, rows_ref) = refs[:columns], refs[columns:-2], refs[-2:]
    owners, channels, own, _ = out_refs[0].shape
    _, pols, _, beams, samples = formed_refs[0].shape
    for c in range(channels):
        for r, formed_ref in enumerate(formed_refs):
            y = me_ref[0] ^ r
            for p in range(pols):
                for a in range(2):
                    rows_ref[p, y, :, a * samples : (a + 1) * samples] = formed_ref[c, p, a]
        rows = rows_ref[...].reshape(pols * columns * beams, 2 * samples)
        spectra = jnp.dot(rows, high_ref[...], preferred_element_type=jnp.float32) + jnp.dot(
            rows, low_ref[...], preferred_element_type=jnp.float32
        )
        real, imag = [], []
        for p in range(pols):
            g = [spectra[(p * columns + y) * beams :][:beams] for y in range(columns)]
            even_sum, even_diff = g[0] + g[2], g[0] - g[2]
            odd_sum, odd_diff = g[1] + g[3], g[1] - g[3]
            zero, two = even_sum + odd_sum, even_sum - odd_sum
            dr, di = even_diff[:, :samples], even_diff[:, samples:]
            qr, qi = odd_diff[:, :samples], odd_diff[:, samples:]
            real.append([zero[:, :samples], dr + qi, two[:, :samples], dr - qi])
            imag.append([zero[:, samples:], di - qr, two[:, samples:], di + qr])
        stokes, total = [], None
        for e in range(columns):
            xr, xi, yr, yi = real[0][e], imag[0][e], real[1][e], imag[1][e]
            intensity = (xr * xr + xi * xi + yr * yr + yi * yi).astype(jnp.bfloat16)
            circular = (2.0 * (xi * yr - xr * yi)).astype(jnp.bfloat16)
            stokes.append(jnp.concatenate([intensity, circular], axis=1))
            part = intensity.astype(jnp.float32)
            total = part if total is None else total + part
        sum_ref[0, c : c + 1, :] = jnp.sum(total, axis=0, keepdims=True)
        ordered = jnp.dot(
            order_ref[...], jnp.concatenate(stokes, axis=0), preferred_element_type=jnp.float32
        )
        for d in range(owners * len(out_refs)):
            block = ordered[d * own : (d + 1) * own].astype(jnp.bfloat16)
            out_refs[d // owners][d % owners, c] = block


def flag_kernel(layout, me_ref, group_ref, common_ref, mask_ref, *refs):
    chunk_refs, out_ref, power_ref = refs[:-2], refs[-2], refs[-1]
    beams, width = chunk_refs[0].shape[2:]
    samples = width // 2
    channels = common_ref.shape[0]
    local = layout[-1][0] + layout[-1][1]
    sources = channels // local

    def blocks(work, carry):
        refs = iter(chunk_refs)
        whole, single = [], []
        for first, size, count in layout:
            if count == 1:
                whole.append((first, size, next(refs)))
            else:
                single.extend((first, size, r, next(refs)) for r in range(count))

        def step(s, carry):
            for first, size, ref in whole:
                carry = work(carry, ref.at[s], s * local + first, size)
            return carry

        carry = lax.fori_loop(0, sources, step, carry)
        for first, size, r, ref in single:
            carry = work(carry, ref.at[0], (me_ref[1] ^ r) * local + first, size)
        return carry

    def measure(level, block_ref, channel, size):
        common = common_ref[pl.ds(channel, size)]
        cleaned = block_ref[:, :, :samples].astype(jnp.float32) - common
        squares = (cleaned * cleaned).reshape(size * beams, samples)
        high = squares.astype(jnp.bfloat16)
        low = (squares - high.astype(jnp.float32)).astype(jnp.bfloat16)
        squares = jnp.concatenate([high, low], axis=1)
        power = jnp.dot(squares, group_ref[...], preferred_element_type=jnp.float32)
        power = power.reshape(size, beams, samples)
        power_ref[pl.ds(channel, size)] = power
        return level + jnp.sum(power, axis=0)

    level = blocks(measure, jnp.zeros((beams, samples), jnp.float32))
    level = jnp.sum(level, axis=1, keepdims=True) / float(channels * samples) + epsilon
    scale = jnp.broadcast_to(0.5 / level, (beams, samples))

    def flag(carry, block_ref, channel, size):
        for c in range(size):
            row = block_ref[c].astype(jnp.float32)
            cleaned = row[:, :samples] - common_ref[channel + c]
            weight = mask_ref[channel + c] / (1.0 + power_ref[channel + c] * scale)
            where = pl.ds(pl.multiple_of((channel + c) * samples, samples), samples)
            out_ref[0, :, where] = (cleaned * weight).astype(jnp.bfloat16)
            out_ref[1, :, where] = (row[:, samples:] * weight).astype(jnp.bfloat16)
        return carry

    blocks(flag, 0)


def whole_spec(array):
    return pl.BlockSpec(array.shape, lambda *_: (0,) * array.ndim)


def form(me, after, table, gains, volts, first, per_chunk, step, groups):
    real, imag = volts
    _, _, pols, feeds, samples = real.shape
    steps = per_chunk // step
    gain_spec = pl.BlockSpec((step, 1, pols, feeds), lambda i: (first // step + i, 0, 0, 0))
    volt_spec = pl.BlockSpec(
        (step, 1, pols, feeds, samples), lambda i: (first // step + i, 0, 0, 0, 0)
    )
    beams = feeds // groups
    return pl.pallas_call(
        form_kernel,
        grid=(steps,),
        in_specs=[
            pl.BlockSpec(memory_space=pltpu.SMEM),
            pl.BlockSpec(memory_space=pl.ANY),
            whole_spec(table),
            gain_spec,
            gain_spec,
            volt_spec,
            volt_spec,
        ],
        out_specs=[pl.BlockSpec((step, pols, 2, beams, samples), lambda i: (i, 0, 0, 0, 0))]
        * groups,
        out_shape=[jax.ShapeDtypeStruct((per_chunk, pols, 2, beams, samples), jnp.bfloat16)]
        * groups,
        scratch_shapes=[pltpu.VMEM((2, 8, feeds), jnp.float32)],
        cost_estimate=pl.CostEstimate(
            flops=1000,
            bytes_accessed=1000,
            transcendentals=0,
        ),
        compiler_params=pltpu.CompilerParams(vmem_limit_bytes=60 << 20),
        name="form",
    )(me, after, table, *gains, real, imag)


def detect(me, tables, order, formed, after, step, owners, direct):
    columns = len(formed)
    per_chunk, pols, _, beams, samples = formed[0].shape
    steps = per_chunk // step
    own = columns * beams // owners
    counts = [1] * owners if direct else [owners]
    block_spec = pl.BlockSpec((step, pols, 2, beams, samples), lambda i: (i, 0, 0, 0, 0))
    return pl.pallas_call(
        functools.partial(detect_kernel, columns, len(after)),
        grid=(steps,),
        in_specs=[
            pl.BlockSpec(memory_space=pltpu.SMEM),
            *[pl.BlockSpec(memory_space=pl.ANY)] * len(after),
            *[whole_spec(table) for table in tables],
            whole_spec(order),
            *[block_spec] * columns,
        ],
        out_specs=[
            *[
                pl.BlockSpec((count, step, own, 2 * samples), lambda i: (0, i, 0, 0))
                for count in counts
            ],
            pl.BlockSpec((1, step, samples), lambda i: (i, 0, 0)),
        ],
        out_shape=[
            *[
                jax.ShapeDtypeStruct((count, per_chunk, own, 2 * samples), jnp.bfloat16)
                for count in counts
            ],
            jax.ShapeDtypeStruct((steps, step, samples), jnp.float32),
        ],
        scratch_shapes=[pltpu.VMEM((pols, columns, beams, 2 * samples), jnp.bfloat16)],
        cost_estimate=pl.CostEstimate(
            flops=per_chunk * DETECT_FLOPS,
            bytes_accessed=1000,
            transcendentals=0,
        ),
        compiler_params=pltpu.CompilerParams(vmem_limit_bytes=60 << 20),
        name="detect",
    )(me, *after, *tables, order, *formed)


def soft_flag(me, owned, common, mask, frame_count):
    own, width = owned[0][0].shape[2:]
    sizes = [one[0].shape[1] for one in owned]
    layout = [(sum(sizes[:i]), sizes[i], len(one)) for i, one in enumerate(owned)]
    owned = [block for one in owned for block in one]
    samples = width // 2
    channels = common.shape[0]
    block = 16 if own % 16 == 0 else own
    group = np.kron(np.eye(samples // frame_count), np.ones((frame_count, frame_count)))
    group = jnp.asarray(np.concatenate([group, group]) / frame_count, jnp.bfloat16)
    return pl.pallas_call(
        functools.partial(flag_kernel, layout),
        grid=(own // block,),
        in_specs=[
            pl.BlockSpec(memory_space=pltpu.SMEM),
            whole_spec(group),
            whole_spec(common),
            whole_spec(mask),
            *[
                pl.BlockSpec((*one.shape[:2], block, width), lambda i: (0, 0, i, 0))
                for one in owned
            ],
        ],
        out_specs=pl.BlockSpec((2, block, channels * samples), lambda i: (0, i, 0)),
        out_shape=jax.ShapeDtypeStruct((2, own, channels * samples), jnp.bfloat16),
        scratch_shapes=[pltpu.VMEM((channels, block, samples), jnp.float32)],
        cost_estimate=pl.CostEstimate(
            flops=channels * own * samples * samples * 4,
            bytes_accessed=channels * own * samples * 8,
            transcendentals=0,
        ),
        compiler_params=pltpu.CompilerParams(vmem_limit_bytes=60 << 20),
        name="flag",
    )(me, group, common, mask, *owned)


def swap(one, axis, apart):
    return lax.ppermute(one, axis, [(i, i ^ apart) for i in range(lax.axis_size(axis))])


def body(voltage_real, voltage_imag, gain_real, gain_imag, channel_mask, beam_owner):
    local, _, pols, feeds, samples = voltage_real.shape
    frame_count = samples // UP
    owners, groups = lax.axis_size("chan"), lax.axis_size("grp")
    channels = local * owners
    unit = local // sum(SHARES)
    sizes = [share * unit for share in SHARES] if local == unit * sum(SHARES) else [1] * local
    chunks = len(sizes)
    firsts = [sum(sizes[:chunk]) for chunk in range(chunks)]
    step = math.gcd(*sizes, 2)

    gains = (gain_real, gain_imag)
    mine = lax.axis_index("grp")
    table = jnp.asarray(beam_table(feeds, groups))
    near = lax.axis_index("chan")
    me = jnp.stack([mine, near]).astype(jnp.int32)
    tables = [jnp.asarray(one) for one in spectral_tables(UP, frame_count, groups)]
    slots = beam_owner.shape[1]
    wanted = beam_owner[0].reshape(owners, slots // owners)
    orders = [
        (one.reshape(slots, 1) == jnp.arange(slots, dtype=jnp.int32)).astype(jnp.bfloat16)
        for one in (wanted, wanted[near ^ jnp.arange(owners, dtype=jnp.int32)])
    ]
    mask = jnp.repeat(channel_mask.astype(jnp.float32), frame_count).reshape(channels, 1, samples)
    volts = (voltage_real, voltage_imag)
    turned, owned, sums = [], [], []
    after = me
    for chunk in range(chunks + 1):
        if chunk < chunks:
            formed = form(
                me, after, table, gains, volts, firsts[chunk], sizes[chunk], step, groups
            )
            turned.append([swap(one, "grp", r) if r else one for r, one in enumerate(formed)])
            after = formed[0]
        if chunk > 0:
            direct = chunks == len(DIRECT) and DIRECT[chunk - 1]
            before = owned[-2] if len(owned) > 1 else []
            *sent, part = detect(
                me,
                tables,
                orders[direct],
                turned[chunk - 1],
                [after, *before],
                step,
                owners,
                direct,
            )
            sums.append(part.reshape(sizes[chunk - 1], samples))
            after = part
            if chunk == chunks:
                common = jnp.concatenate(sums, axis=0).reshape(groups, local // groups, samples)
                parts = [common[mine ^ r] for r in range(groups)]
                common = parts[0]
                for r in range(1, groups):
                    common = common + swap(parts[r], "grp", r)
                common = common / float(feeds * groups)
                common_piece = common.reshape(-1)
                common, *sent = lax.optimization_barrier((common, *sent))
            if direct:
                owned.append([swap(one, "chan", r) if r else one for r, one in enumerate(sent)])
            else:
                owned.append([lax.all_to_all(*sent, "chan", split_axis=0, concat_axis=0, tiled=True)])
    shared = jnp.zeros((owners, local // groups, samples), jnp.float32)
    for r in range(owners):
        other = swap(common, "chan", r) if r else common
        shared = lax.dynamic_update_index_in_dim(shared, other, near ^ r, 0)
    common = jnp.zeros((owners, groups, local // groups, samples), jnp.float32)
    for r in range(groups):
        other = swap(shared, "grp", r) if r else shared
        common = lax.dynamic_update_index_in_dim(common, other, mine ^ r, 1)
    flagged = soft_flag(me, owned, common.reshape(channels, 1, samples), mask, frame_count)
    return (flagged, common_piece)


def solution(mesh):
    in_specs = (
        P("chan", "grp", None, None, None),
        P("chan", "grp", None, None, None),
        P("chan", "grp", None, None),
        P("chan", "grp", None, None),
        P(),
        P("grp", None),
    )
    out_specs = (P(None, ("chan", "grp"), None), P(("chan", "grp")))
    return jax.shard_map(body, mesh=mesh, in_specs=in_specs, out_specs=out_specs, check_vma=False)
```

```python
import functools
import math

import jax
import jax.numpy as jnp
import numpy as np
from jax import lax
from jax.experimental import pallas as pl
from jax.experimental.pallas import tpu as pltpu
from jax.sharding import PartitionSpec as P

UP = 16
SHARES = (2,3,4,5,5,6,7)
DIRECT = (False,) * 7
DETECT_FLOPS = 1750000000

epsilon = 1e-05


def beam_table(feed_count, group_count):
    counter = np.arange(feed_count)
    angles = (counter[:, None] * counter[None, :] % feed_count) * (-2.0 * math.pi / feed_count)
    factor = 1.0 / math.sqrt(feed_count)
    cosine, sines = np.cos(angles) * factor, np.sin(angles) * factor
    table = np.stack([np.concatenate([cosine, -sines], 1), np.concatenate([sines, cosine], 1)])
    table = table.reshape(2, group_count, feed_count // group_count, 2 * feed_count)
    table = table.swapaxes(0, 1).reshape(group_count, -1, 2 * feed_count)
    return table.astype(np.float32).astype(jnp.bfloat16)


def spectral_tables(up_count, frame_count, column_count):
    spectral = np.arange(up_count)
    angles = (spectral[:, None] * spectral[None, :] % up_count) * (-2.0 * math.pi / up_count)
    factor = 1.0 / math.sqrt(column_count * up_count)
    cosine, sines = np.cos(angles) * factor, np.sin(angles) * factor
    same = np.eye(frame_count)
    sample_count = frame_count * up_count

    def spread(entries):
        return np.einsum("uk,tv->tukv", entries, same).reshape(sample_count, sample_count)

    table = np.block([[spread(cosine), spread(sines)], [-spread(sines), spread(cosine)]])
    table = table.astype(np.float32)
    high = table.astype(jnp.bfloat16)
    low = (table - high.astype(np.float32)).astype(jnp.bfloat16)
    return high, low


def form_kernel(me_ref, after_ref, table_ref, gain_real_ref, gain_imag_ref, real_ref, imag_ref, *refs):
    out_refs, gains_ref = refs[:-1], refs[-1]
    channels, pols, _, beams, samples = out_refs[0].shape
    for c in range(channels):
        gains_ref[0, c * pols : (c + 1) * pols] = gain_real_ref[c, 0]
        gains_ref[1, c * pols : (c + 1) * pols] = gain_imag_ref[c, 0]
    gains_real, gains_imag = gains_ref[0].T, gains_ref[1].T
    table = jnp.concatenate([table_ref[me_ref[0] ^ r] for r in range(len(out_refs))], axis=0)
    for c in range(channels):
        columns = []
        for p in range(pols):
            j = c * pols + p
            gain_real, gain_imag = gains_real[:, j : j + 1], gains_imag[:, j : j + 1]
            real = real_ref[c, 0, p].astype(jnp.float32)
            imag = imag_ref[c, 0, p].astype(jnp.float32)
            real_part = (gain_real * real - gain_imag * imag).astype(jnp.bfloat16)
            imag_part = (gain_real * imag + gain_imag * real).astype(jnp.bfloat16)
            columns.append(jnp.concatenate([real_part, imag_part], axis=0))
        calibrated = jnp.concatenate(columns, axis=1)
        formed = jnp.dot(table, calibrated, preferred_element_type=jnp.float32)
        formed = formed.astype(jnp.bfloat16)
        for p in range(pols):
            for r, out_ref in enumerate(out_refs):
                for a in range(2):
                    row = (r * 2 + a) * beams
                    out_ref[c, p, a] = formed[row : row + beams, p * samples : (p + 1) * samples]


def detect_kernel(columns, me_ref, after_ref, before_ref, high_ref, low_ref, order_ref, *refs):
    formed_refs, out_refs, (sum_ref, rows_ref) = refs[:columns], refs[columns:-2], refs[-2:]
    owners, channels, own, _ = out_refs[0].shape
    _, pols, _, beams, samples = formed_refs[0].shape
    for c in range(channels):
        for r, formed_ref in enumerate(formed_refs):
            y = me_ref[0] ^ r
            for p in range(pols):
                for a in range(2):
                    rows_ref[p, y, :, a * samples : (a + 1) * samples] = formed_ref[c, p, a]
        rows = rows_ref[...].reshape(pols * columns * beams, 2 * samples)
        spectra = jnp.dot(rows, high_ref[...], preferred_element_type=jnp.float32) + jnp.dot(
            rows, low_ref[...], preferred_element_type=jnp.float32
        )
        real, imag = [], []
        for p in range(pols):
            g = [spectra[(p * columns + y) * beams :][:beams] for y in range(columns)]
            even_sum, even_diff = g[0] + g[2], g[0] - g[2]
            odd_sum, odd_diff = g[1] + g[3], g[1] - g[3]
            zero, two = even_sum + odd_sum, even_sum - odd_sum
            dr, di = even_diff[:, :samples], even_diff[:, samples:]
            qr, qi = odd_diff[:, :samples], odd_diff[:, samples:]
            real.append([zero[:, :samples], dr + qi, two[:, :samples], dr - qi])
            imag.append([zero[:, samples:], di - qr, two[:, samples:], di + qr])
        stokes, total = [], None
        for e in range(columns):
            xr, xi, yr, yi = real[0][e], imag[0][e], real[1][e], imag[1][e]
            intensity = (xr * xr + xi * xi + yr * yr + yi * yi).astype(jnp.bfloat16)
            circular = (2.0 * (xi * yr - xr * yi)).astype(jnp.bfloat16)
            stokes.append(jnp.concatenate([intensity, circular], axis=1))
            part = intensity.astype(jnp.float32)
            total = part if total is None else total + part
        sum_ref[0, c : c + 1, :] = jnp.sum(total, axis=0, keepdims=True)
        ordered = jnp.dot(
            order_ref[...], jnp.concatenate(stokes, axis=0), preferred_element_type=jnp.float32
        )
        for d in range(owners * len(out_refs)):
            block = ordered[d * own : (d + 1) * own].astype(jnp.bfloat16)
            out_refs[d // owners][d % owners, c] = block


def flag_kernel(layout, me_ref, group_ref, common_ref, mask_ref, *refs):
    chunk_refs, out_ref, power_ref = refs[:-2], refs[-2], refs[-1]
    beams, width = chunk_refs[0].shape[2:]
    samples = width // 2
    channels = common_ref.shape[0]
    local = layout[-1][0] + layout[-1][1]
    sources = channels // local

    def blocks(work, carry):
        refs = iter(chunk_refs)
        whole, single = [], []
        for first, size, count in layout:
            if count == 1:
                whole.append((first, size, next(refs)))
            else:
                single.extend((first, size, r, next(refs)) for r in range(count))

        def step(s, carry):
            for first, size, ref in whole:
                carry = work(carry, ref.at[s], s * local + first, size)
            return carry

        carry = lax.fori_loop(0, sources, step, carry)
        for first, size, r, ref in single:
            carry = work(carry, ref.at[0], (me_ref[1] ^ r) * local + first, size)
        return carry

    def measure(level, block_ref, channel, size):
        common = common_ref[pl.ds(channel, size)]
        cleaned = block_ref[:, :, :samples].astype(jnp.float32) - common
        squares = (cleaned * cleaned).reshape(size * beams, samples)
        high = squares.astype(jnp.bfloat16)
        low = (squares - high.astype(jnp.float32)).astype(jnp.bfloat16)
        squares = jnp.concatenate([high, low], axis=1)
        power = jnp.dot(squares, group_ref[...], preferred_element_type=jnp.float32)
        power = power.reshape(size, beams, samples)
        power_ref[pl.ds(channel, size)] = power
        return level + jnp.sum(power, axis=0)

    level = blocks(measure, jnp.zeros((beams, samples), jnp.float32))
    level = jnp.sum(level, axis=1, keepdims=True) / float(channels * samples) + epsilon
    scale = jnp.broadcast_to(0.5 / level, (beams, samples))

    def flag(carry, block_ref, channel, size):
        for c in range(size):
            row = block_ref[c].astype(jnp.float32)
            cleaned = row[:, :samples] - common_ref[channel + c]
            weight = mask_ref[channel + c] / (1.0 + power_ref[channel + c] * scale)
            where = pl.ds(pl.multiple_of((channel + c) * samples, samples), samples)
            out_ref[0, :, where] = (cleaned * weight).astype(jnp.bfloat16)
            out_ref[1, :, where] = (row[:, samples:] * weight).astype(jnp.bfloat16)
        return carry

    blocks(flag, 0)


def whole_spec(array):
    return pl.BlockSpec(array.shape, lambda *_: (0,) * array.ndim)


def form(me, after, table, gains, volts, first, per_chunk, step, groups):
    real, imag = volts
    _, _, pols, feeds, samples = real.shape
    steps = per_chunk // step
    gain_spec = pl.BlockSpec((step, 1, pols, feeds), lambda i: (first // step + i, 0, 0, 0))
    volt_spec = pl.BlockSpec(
        (step, 1, pols, feeds, samples), lambda i: (first // step + i, 0, 0, 0, 0)
    )
    beams = feeds // groups
    return pl.pallas_call(
        form_kernel,
        grid=(steps,),
        in_specs=[
            pl.BlockSpec(memory_space=pltpu.SMEM),
            pl.BlockSpec(memory_space=pl.ANY),
            whole_spec(table),
            gain_spec,
            gain_spec,
            volt_spec,
            volt_spec,
        ],
        out_specs=[pl.BlockSpec((step, pols, 2, beams, samples), lambda i: (i, 0, 0, 0, 0))]
        * groups,
        out_shape=[jax.ShapeDtypeStruct((per_chunk, pols, 2, beams, samples), jnp.bfloat16)]
        * groups,
        scratch_shapes=[pltpu.VMEM((2, 8, feeds), jnp.float32)],
        cost_estimate=pl.CostEstimate(
            flops=1000,
            bytes_accessed=1000,
            transcendentals=0,
        ),
        compiler_params=pltpu.CompilerParams(vmem_limit_bytes=60 << 20),
        name="form",
    )(me, after, table, *gains, real, imag)


def detect(me, tables, order, formed, after, step, owners, direct):
    columns = len(formed)
    per_chunk, pols, _, beams, samples = formed[0].shape
    steps = per_chunk // step
    own = columns * beams // owners
    counts = [1] * owners if direct else [owners]
    block_spec = pl.BlockSpec((step, pols, 2, beams, samples), lambda i: (i, 0, 0, 0, 0))
    return pl.pallas_call(
        functools.partial(detect_kernel, columns),
        grid=(steps,),
        in_specs=[
            pl.BlockSpec(memory_space=pltpu.SMEM),
            pl.BlockSpec(memory_space=pl.ANY),
            pl.BlockSpec(memory_space=pl.ANY),
            *[whole_spec(table) for table in tables],
            whole_spec(order),
            *[block_spec] * columns,
        ],
        out_specs=[
            *[
                pl.BlockSpec((count, step, own, 2 * samples), lambda i: (0, i, 0, 0))
                for count in counts
            ],
            pl.BlockSpec((1, step, samples), lambda i: (i, 0, 0)),
        ],
        out_shape=[
            *[
                jax.ShapeDtypeStruct((count, per_chunk, own, 2 * samples), jnp.bfloat16)
                for count in counts
            ],
            jax.ShapeDtypeStruct((steps, step, samples), jnp.float32),
        ],
        scratch_shapes=[pltpu.VMEM((pols, columns, beams, 2 * samples), jnp.bfloat16)],
        cost_estimate=pl.CostEstimate(
            flops=per_chunk * DETECT_FLOPS,
            bytes_accessed=1000,
            transcendentals=0,
        ),
        compiler_params=pltpu.CompilerParams(vmem_limit_bytes=60 << 20),
        name="detect",
    )(me, *after, *tables, order, *formed)


def soft_flag(me, owned, common, mask, frame_count):
    own, width = owned[0][0].shape[2:]
    sizes = [one[0].shape[1] for one in owned]
    layout = [(sum(sizes[:i]), sizes[i], len(one)) for i, one in enumerate(owned)]
    owned = [block for one in owned for block in one]
    samples = width // 2
    channels = common.shape[0]
    block = 16 if own % 16 == 0 else own
    group = np.kron(np.eye(samples // frame_count), np.ones((frame_count, frame_count)))
    group = jnp.asarray(np.concatenate([group, group]) / frame_count, jnp.bfloat16)
    return pl.pallas_call(
        functools.partial(flag_kernel, layout),
        grid=(own // block,),
        in_specs=[
            pl.BlockSpec(memory_space=pltpu.SMEM),
            whole_spec(group),
            whole_spec(common),
            whole_spec(mask),
            *[
                pl.BlockSpec((*one.shape[:2], block, width), lambda i: (0, 0, i, 0))
                for one in owned
            ],
        ],
        out_specs=pl.BlockSpec((2, block, channels * samples), lambda i: (0, i, 0)),
        out_shape=jax.ShapeDtypeStruct((2, own, channels * samples), jnp.bfloat16),
        scratch_shapes=[pltpu.VMEM((channels, block, samples), jnp.float32)],
        cost_estimate=pl.CostEstimate(
            flops=channels * own * samples * samples * 4,
            bytes_accessed=channels * own * samples * 8,
            transcendentals=0,
        ),
        compiler_params=pltpu.CompilerParams(vmem_limit_bytes=60 << 20),
        name="flag",
    )(me, group, common, mask, *owned)


def swap(one, axis, apart):
    return lax.ppermute(one, axis, [(i, i ^ apart) for i in range(lax.axis_size(axis))])


def body(voltage_real, voltage_imag, gain_real, gain_imag, channel_mask, beam_owner):
    local, _, pols, feeds, samples = voltage_real.shape
    frame_count = samples // UP
    owners, groups = lax.axis_size("chan"), lax.axis_size("grp")
    channels = local * owners
    unit = local // sum(SHARES)
    sizes = [share * unit for share in SHARES] if local == unit * sum(SHARES) else [1] * local
    chunks = len(sizes)
    firsts = [sum(sizes[:chunk]) for chunk in range(chunks)]
    step = math.gcd(*sizes, 2)

    gains = (gain_real, gain_imag)
    mine = lax.axis_index("grp")
    table = jnp.asarray(beam_table(feeds, groups))
    near = lax.axis_index("chan")
    me = jnp.stack([mine, near]).astype(jnp.int32)
    tables = [jnp.asarray(one) for one in spectral_tables(UP, frame_count, groups)]
    slots = beam_owner.shape[1]
    wanted = beam_owner[0].reshape(owners, slots // owners)
    orders = [
        (one.reshape(slots, 1) == jnp.arange(slots, dtype=jnp.int32)).astype(jnp.bfloat16)
        for one in (wanted, wanted[near ^ jnp.arange(owners, dtype=jnp.int32)])
    ]
    mask = jnp.repeat(channel_mask.astype(jnp.float32), frame_count).reshape(channels, 1, samples)
    volts = (voltage_real, voltage_imag)
    turned, owned, sums = [], [], []
    after = me
    for chunk in range(chunks + 1):
        if chunk < chunks:
            formed = form(
                me, after, table, gains, volts, firsts[chunk], sizes[chunk], step, groups
            )
            turned.append([swap(one, "grp", r) if r else one for r, one in enumerate(formed)])
            after = formed[0]
        if chunk > 0:
            direct = chunks == len(DIRECT) and DIRECT[chunk - 1]
            before = owned[-2][-1] if len(owned) > 1 else me
            *sent, part = detect(
                me,
                tables,
                orders[direct],
                turned[chunk - 1],
                [after, before],
                step,
                owners,
                direct,
            )
            if direct:
                owned.append([swap(one, "chan", r) if r else one for r, one in enumerate(sent)])
            else:
                owned.append([lax.all_to_all(*sent, "chan", split_axis=0, concat_axis=0, tiled=True)])
            sums.append(part.reshape(sizes[chunk - 1], samples))
            after = part
    common = jnp.concatenate(sums, axis=0).reshape(groups, local // groups, samples)
    mine_of = [common[mine ^ r] for r in range(groups)]
    common = mine_of[0]
    for r in range(1, groups):
        common = common + swap(mine_of[r], "grp", r)
    common = common / float(feeds * groups)
    common_piece = common.reshape(-1)
    shared = common[None]
    for bit in range(owners.bit_length() - 1):
        other = swap(shared, "chan", 1 << bit)
        low = (near >> bit) % 2 == 0
        shared = jnp.where(low, jnp.stack([shared, other]), jnp.stack([other, shared]))
        shared = shared.reshape(-1, local // groups, samples)
    common = jnp.zeros((owners, groups, local // groups, samples), jnp.float32)
    for r in range(groups):
        other = swap(shared, "grp", r) if r else shared
        common = lax.dynamic_update_index_in_dim(common, other, mine ^ r, 1)
    flagged = soft_flag(me, owned, common.reshape(channels, 1, samples), mask, frame_count)
    return (flagged, common_piece)


def solution(mesh):
    in_specs = (
        P("chan", "grp", None, None, None),
        P("chan", "grp", None, None, None),
        P("chan", "grp", None, None),
        P("chan", "grp", None, None),
        P(),
        P("grp", None),
    )
    out_specs = (P(None, ("chan", "grp"), None), P(("chan", "grp")))
    return jax.shard_map(body, mesh=mesh, in_specs=in_specs, out_specs=out_specs, check_vma=False)
```

```python
import functools
import math

import jax
import jax.numpy as jnp
import numpy as np
from jax import lax
from jax.experimental import pallas as pl
from jax.experimental.pallas import tpu as pltpu
from jax.sharding import PartitionSpec as P

UP = 16
SHARES = (2, 4, 5, 6, 7, 8)
DIRECT = (False,) * 6
DETECT_FLOPS = 1_600_000_000

epsilon = 1e-05


def beam_table(feed_count, group_count):
    counter = np.arange(feed_count)
    angles = (counter[:, None] * counter[None, :] % feed_count) * (-2.0 * math.pi / feed_count)
    factor = 1.0 / math.sqrt(feed_count)
    cosine, sines = np.cos(angles) * factor, np.sin(angles) * factor
    table = np.stack([np.concatenate([cosine, -sines], 1), np.concatenate([sines, cosine], 1)])
    table = table.reshape(2, group_count, feed_count // group_count, 2 * feed_count)
    table = table.swapaxes(0, 1).reshape(group_count, -1, 2 * feed_count)
    return table.astype(np.float32).astype(jnp.bfloat16)


def spectral_tables(up_count, frame_count, column_count):
    spectral = np.arange(up_count)
    angles = (spectral[:, None] * spectral[None, :] % up_count) * (-2.0 * math.pi / up_count)
    factor = 1.0 / math.sqrt(column_count * up_count)
    cosine, sines = np.cos(angles) * factor, np.sin(angles) * factor
    same = np.eye(frame_count)
    sample_count = frame_count * up_count

    def spread(entries):
        return np.einsum("uk,tv->tukv", entries, same).reshape(sample_count, sample_count)

    table = np.block([[spread(cosine), spread(sines)], [-spread(sines), spread(cosine)]])
    table = table.astype(np.float32)
    high = table.astype(jnp.bfloat16)
    low = (table - high.astype(np.float32)).astype(jnp.bfloat16)
    return high, low


def form_kernel(me_ref, after_ref, table_ref, gain_real_ref, gain_imag_ref, real_ref, imag_ref, *refs):
    out_refs, gains_ref = refs[:-1], refs[-1]
    channels, pols, _, beams, samples = out_refs[0].shape
    for c in range(channels):
        gains_ref[0, c * pols : (c + 1) * pols] = gain_real_ref[c, 0]
        gains_ref[1, c * pols : (c + 1) * pols] = gain_imag_ref[c, 0]
    gains_real, gains_imag = gains_ref[0].T, gains_ref[1].T
    table = jnp.concatenate([table_ref[me_ref[0] ^ r] for r in range(len(out_refs))], axis=0)
    for c in range(channels):
        columns = []
        for p in range(pols):
            j = c * pols + p
            gain_real, gain_imag = gains_real[:, j : j + 1], gains_imag[:, j : j + 1]
            real = real_ref[c, 0, p].astype(jnp.float32)
            imag = imag_ref[c, 0, p].astype(jnp.float32)
            real_part = (gain_real * real - gain_imag * imag).astype(jnp.bfloat16)
            imag_part = (gain_real * imag + gain_imag * real).astype(jnp.bfloat16)
            columns.append(jnp.concatenate([real_part, imag_part], axis=0))
        calibrated = jnp.concatenate(columns, axis=1)
        formed = jnp.dot(table, calibrated, preferred_element_type=jnp.float32)
        formed = formed.astype(jnp.bfloat16)
        for p in range(pols):
            for r, out_ref in enumerate(out_refs):
                for a in range(2):
                    row = (r * 2 + a) * beams
                    out_ref[c, p, a] = formed[row : row + beams, p * samples : (p + 1) * samples]


def detect_kernel(columns, me_ref, after_ref, before_ref, high_ref, low_ref, order_ref, *refs):
    formed_refs, out_refs, (sum_ref, rows_ref) = refs[:columns], refs[columns:-2], refs[-2:]
    owners, channels, own, _ = out_refs[0].shape
    _, pols, _, beams, samples = formed_refs[0].shape
    for c in range(channels):
        for r, formed_ref in enumerate(formed_refs):
            y = me_ref[0] ^ r
            for p in range(pols):
                for a in range(2):
                    rows_ref[p, y, :, a * samples : (a + 1) * samples] = formed_ref[c, p, a]
        rows = rows_ref[...].reshape(pols * columns * beams, 2 * samples)
        spectra = jnp.dot(rows, high_ref[...], preferred_element_type=jnp.float32) + jnp.dot(
            rows, low_ref[...], preferred_element_type=jnp.float32
        )
        real, imag = [], []
        for p in range(pols):
            g = [spectra[(p * columns + y) * beams :][:beams] for y in range(columns)]
            even_sum, even_diff = g[0] + g[2], g[0] - g[2]
            odd_sum, odd_diff = g[1] + g[3], g[1] - g[3]
            zero, two = even_sum + odd_sum, even_sum - odd_sum
            dr, di = even_diff[:, :samples], even_diff[:, samples:]
            qr, qi = odd_diff[:, :samples], odd_diff[:, samples:]
            real.append([zero[:, :samples], dr + qi, two[:, :samples], dr - qi])
            imag.append([zero[:, samples:], di - qr, two[:, samples:], di + qr])
        stokes, total = [], None
        for e in range(columns):
            xr, xi, yr, yi = real[0][e], imag[0][e], real[1][e], imag[1][e]
            intensity = (xr * xr + xi * xi + yr * yr + yi * yi).astype(jnp.bfloat16)
            circular = (2.0 * (xi * yr - xr * yi)).astype(jnp.bfloat16)
            stokes.append(jnp.concatenate([intensity, circular], axis=1))
            part = intensity.astype(jnp.float32)
            total = part if total is None else total + part
        sum_ref[0, c : c + 1, :] = jnp.sum(total, axis=0, keepdims=True)
        ordered = jnp.dot(
            order_ref[...], jnp.concatenate(stokes, axis=0), preferred_element_type=jnp.float32
        )
        for d in range(owners * len(out_refs)):
            block = ordered[d * own : (d + 1) * own].astype(jnp.bfloat16)
            out_refs[d // owners][d % owners, c] = block


def flag_kernel(layout, groups, me_ref, group_ref, mask_ref, *refs):
    part_refs, chunk_refs = refs[:groups], refs[groups:-3]
    out_ref, power_ref, common_ref = refs[-3:]
    beams, width = chunk_refs[0].shape[2:]
    samples = width // 2
    channels = common_ref.shape[0]
    local = layout[-1][0] + layout[-1][1]
    sources = channels // local

    @pl.when(pl.program_id(0) == 0)
    def _():
        part = local // groups

        def place(s, carry):
            for r, part_ref in enumerate(part_refs):
                first = s * local + (me_ref[0] ^ r) * part
                common_ref[pl.ds(first, part)] = part_ref[s]
            return carry

        lax.fori_loop(0, sources, place, 0)

    def blocks(work, carry):
        refs = iter(chunk_refs)
        whole, single = [], []
        for first, size, count in layout:
            if count == 1:
                whole.append((first, size, next(refs)))
            else:
                single.extend((first, size, r, next(refs)) for r in range(count))

        def step(s, carry):
            for first, size, ref in whole:
                carry = work(carry, ref.at[s], s * local + first, size)
            return carry

        carry = lax.fori_loop(0, sources, step, carry)
        for first, size, r, ref in single:
            carry = work(carry, ref.at[0], (me_ref[1] ^ r) * local + first, size)
        return carry

    def measure(level, block_ref, channel, size):
        common = common_ref[pl.ds(channel, size)]
        cleaned = block_ref[:, :, :samples].astype(jnp.float32) - common
        squares = (cleaned * cleaned).reshape(size * beams, samples)
        high = squares.astype(jnp.bfloat16)
        low = (squares - high.astype(jnp.float32)).astype(jnp.bfloat16)
        squares = jnp.concatenate([high, low], axis=1)
        power = jnp.dot(squares, group_ref[...], preferred_element_type=jnp.float32)
        power = power.reshape(size, beams, samples)
        power_ref[pl.ds(channel, size)] = power
        return level + jnp.sum(power, axis=0)

    level = blocks(measure, jnp.zeros((beams, samples), jnp.float32))
    level = jnp.sum(level, axis=1, keepdims=True) / float(channels * samples) + epsilon
    scale = jnp.broadcast_to(0.5 / level, (beams, samples))

    def flag(carry, block_ref, channel, size):
        for c in range(size):
            row = block_ref[c].astype(jnp.float32)
            cleaned = row[:, :samples] - common_ref[channel + c]
            weight = mask_ref[channel + c] * pl.reciprocal(1.0 + power_ref[channel + c] * scale)
            where = pl.ds(pl.multiple_of((channel + c) * samples, samples), samples)
            out_ref[0, :, where] = (cleaned * weight).astype(jnp.bfloat16)
            out_ref[1, :, where] = (row[:, samples:] * weight).astype(jnp.bfloat16)
        return carry

    blocks(flag, 0)


def whole_spec(array):
    return pl.BlockSpec(array.shape, lambda *_: (0,) * array.ndim)


def form(me, after, table, gains, volts, first, per_chunk, step, groups):
    real, imag = volts
    _, _, pols, feeds, samples = real.shape
    steps = per_chunk // step
    gain_spec = pl.BlockSpec((step, 1, pols, feeds), lambda i: (first // step + i, 0, 0, 0))
    volt_spec = pl.BlockSpec(
        (step, 1, pols, feeds, samples), lambda i: (first // step + i, 0, 0, 0, 0)
    )
    beams = feeds // groups
    return pl.pallas_call(
        form_kernel,
        grid=(steps,),
        in_specs=[
            pl.BlockSpec(memory_space=pltpu.SMEM),
            pl.BlockSpec(memory_space=pl.ANY),
            whole_spec(table),
            gain_spec,
            gain_spec,
            volt_spec,
            volt_spec,
        ],
        out_specs=[pl.BlockSpec((step, pols, 2, beams, samples), lambda i: (i, 0, 0, 0, 0))]
        * groups,
        out_shape=[jax.ShapeDtypeStruct((per_chunk, pols, 2, beams, samples), jnp.bfloat16)]
        * groups,
        scratch_shapes=[pltpu.VMEM((2, 8, feeds), jnp.float32)],
        cost_estimate=pl.CostEstimate(
            flops=1000,
            bytes_accessed=1000,
            transcendentals=0,
        ),
        compiler_params=pltpu.CompilerParams(vmem_limit_bytes=60 << 20),
        name="form",
    )(me, after, table, *gains, real, imag)


def detect(me, tables, order, formed, after, step, owners, direct):
    columns = len(formed)
    per_chunk, pols, _, beams, samples = formed[0].shape
    steps = per_chunk // step
    own = columns * beams // owners
    counts = [1] * owners if direct else [owners]
    block_spec = pl.BlockSpec((step, pols, 2, beams, samples), lambda i: (i, 0, 0, 0, 0))
    return pl.pallas_call(
        functools.partial(detect_kernel, columns),
        grid=(steps,),
        in_specs=[
            pl.BlockSpec(memory_space=pltpu.SMEM),
            pl.BlockSpec(memory_space=pl.ANY),
            pl.BlockSpec(memory_space=pl.ANY),
            *[whole_spec(table) for table in tables],
            whole_spec(order),
            *[block_spec] * columns,
        ],
        out_specs=[
            *[
                pl.BlockSpec((count, step, own, 2 * samples), lambda i: (0, i, 0, 0))
                for count in counts
            ],
            pl.BlockSpec((1, step, samples), lambda i: (i, 0, 0)),
        ],
        out_shape=[
            *[
                jax.ShapeDtypeStruct((count, per_chunk, own, 2 * samples), jnp.bfloat16)
                for count in counts
            ],
            jax.ShapeDtypeStruct((steps, step, samples), jnp.float32),
        ],
        scratch_shapes=[pltpu.VMEM((pols, columns, beams, 2 * samples), jnp.bfloat16)],
        cost_estimate=pl.CostEstimate(
            flops=per_chunk * DETECT_FLOPS,
            bytes_accessed=1000,
            transcendentals=0,
        ),
        compiler_params=pltpu.CompilerParams(vmem_limit_bytes=60 << 20),
        name="detect",
    )(me, *after, *tables, order, *formed)


def soft_flag(me, owned, parts, mask, frame_count):
    own, width = owned[0][0].shape[2:]
    sizes = [one[0].shape[1] for one in owned]
    layout = [(sum(sizes[:i]), sizes[i], len(one)) for i, one in enumerate(owned)]
    owned = [block for one in owned for block in one]
    samples = width // 2
    channels = mask.shape[0]
    block = 16 if own % 16 == 0 else own
    group = np.kron(np.eye(samples // frame_count), np.ones((frame_count, frame_count)))
    group = jnp.asarray(np.concatenate([group, group]) / frame_count, jnp.bfloat16)
    return pl.pallas_call(
        functools.partial(flag_kernel, layout, len(parts)),
        grid=(own // block,),
        in_specs=[
            pl.BlockSpec(memory_space=pltpu.SMEM),
            whole_spec(group),
            whole_spec(mask),
            *[whole_spec(part) for part in parts],
            *[
                pl.BlockSpec((*one.shape[:2], block, width), lambda i: (0, 0, i, 0))
                for one in owned
            ],
        ],
        out_specs=pl.BlockSpec((2, block, channels * samples), lambda i: (0, i, 0)),
        out_shape=jax.ShapeDtypeStruct((2, own, channels * samples), jnp.bfloat16),
        scratch_shapes=[
            pltpu.VMEM((channels, block, samples), jnp.float32),
            pltpu.VMEM((channels, 1, samples), jnp.float32),
        ],
        cost_estimate=pl.CostEstimate(
            flops=channels * own * samples * samples * 4,
            bytes_accessed=channels * own * samples * 8,
            transcendentals=0,
        ),
        compiler_params=pltpu.CompilerParams(vmem_limit_bytes=60 << 20),
        name="flag",
    )(me, group, mask, *parts, *owned)


def swap(one, axis, apart):
    return lax.ppermute(one, axis, [(i, i ^ apart) for i in range(lax.axis_size(axis))])


def body(voltage_real, voltage_imag, gain_real, gain_imag, channel_mask, beam_owner):
    local, _, pols, feeds, samples = voltage_real.shape
    frame_count = samples // UP
    owners, groups = lax.axis_size("chan"), lax.axis_size("grp")
    channels = local * owners
    unit = local // sum(SHARES)
    sizes = [share * unit for share in SHARES] if local == unit * sum(SHARES) else [1] * local
    chunks = len(sizes)
    firsts = [sum(sizes[:chunk]) for chunk in range(chunks)]
    step = math.gcd(*sizes, 2)

    gains = (gain_real, gain_imag)
    mine = lax.axis_index("grp")
    table = jnp.asarray(beam_table(feeds, groups))
    near = lax.axis_index("chan")
    me = jnp.stack([mine, near]).astype(jnp.int32)
    tables = [jnp.asarray(one) for one in spectral_tables(UP, frame_count, groups)]
    slots = beam_owner.shape[1]
    wanted = beam_owner[0].reshape(owners, slots // owners)
    orders = [
        (one.reshape(slots, 1) == jnp.arange(slots, dtype=jnp.int32)).astype(jnp.bfloat16)
        for one in (wanted, wanted[near ^ jnp.arange(owners, dtype=jnp.int32)])
    ]
    mask = jnp.repeat(channel_mask.astype(jnp.float32), frame_count).reshape(channels, 1, samples)
    volts = (voltage_real, voltage_imag)
    turned, owned, sums = [], [], []
    after = me
    for chunk in range(chunks + 1):
        if chunk < chunks:
            formed = form(
                me, after, table, gains, volts, firsts[chunk], sizes[chunk], step, groups
            )
            turned.append([swap(one, "grp", r) if r else one for r, one in enumerate(formed)])
            after = formed[0]
        if chunk > 0:
            direct = chunks == len(DIRECT) and DIRECT[chunk - 1]
            before = owned[-2][-1] if len(owned) > 1 else me
            *sent, part = detect(
                me,
                tables,
                orders[direct],
                turned[chunk - 1],
                [after, before],
                step,
                owners,
                direct,
            )
            if direct:
                owned.append([swap(one, "chan", r) if r else one for r, one in enumerate(sent)])
            else:
                owned.append([lax.all_to_all(*sent, "chan", split_axis=0, concat_axis=0, tiled=True)])
            sums.append(part.reshape(sizes[chunk - 1], samples))
            after = part
    common = jnp.concatenate(sums, axis=0).reshape(groups, local // groups, samples)
    mine_of = [common[mine ^ r] for r in range(groups)]
    common = mine_of[0]
    for r in range(1, groups):
        common = common + swap(mine_of[r], "grp", r)
    common = common / float(feeds * groups)
    common_piece = common.reshape(-1)
    shared = common[None]
    for bit in range(owners.bit_length() - 1):
        other = swap(shared, "chan", 1 << bit)
        low = (near >> bit) % 2 == 0
        shared = jnp.where(low, jnp.stack([shared, other]), jnp.stack([other, shared]))
        shared = shared.reshape(-1, local // groups, samples)
    shared = shared[:, :, None]
    shared = [swap(shared, "grp", r) if r else shared for r in range(groups)]
    flagged = soft_flag(me, owned, shared, mask, frame_count)
    return (flagged, common_piece)


def solution(mesh):
    in_specs = (
        P("chan", "grp", None, None, None),
        P("chan", "grp", None, None, None),
        P("chan", "grp", None, None),
        P("chan", "grp", None, None),
        P(),
        P("grp", None),
    )
    out_specs = (P(None, ("chan", "grp"), None), P(("chan", "grp")))
    return jax.shard_map(body, mesh=mesh, in_specs=in_specs, out_specs=out_specs, check_vma=False)
```

```python
import functools
import math

import jax
import jax.numpy as jnp
import numpy as np
from jax import lax
from jax.experimental import pallas as pl
from jax.experimental.pallas import tpu as pltpu
from jax.sharding import PartitionSpec as P

UP = 16
SHARES = (2, 4, 5, 6, 7, 8)
DIRECT = (False,) * 6
DETECT_FLOPS = 1_600_000_000

epsilon = 1e-05


def beam_table(feed_count, group_count):
    counter = np.arange(feed_count)
    angles = (counter[:, None] * counter[None, :] % feed_count) * (-2.0 * math.pi / feed_count)
    factor = 1.0 / math.sqrt(feed_count)
    cosine, sines = np.cos(angles) * factor, np.sin(angles) * factor
    table = np.stack([np.concatenate([cosine, -sines], 1), np.concatenate([sines, cosine], 1)])
    table = table.reshape(2, group_count, feed_count // group_count, 2 * feed_count)
    table = table.swapaxes(0, 1).reshape(group_count, -1, 2 * feed_count)
    return table.astype(np.float32).astype(jnp.bfloat16)


def spectral_tables(up_count, frame_count, column_count):
    spectral = np.arange(up_count)
    angles = (spectral[:, None] * spectral[None, :] % up_count) * (-2.0 * math.pi / up_count)
    factor = 1.0 / math.sqrt(column_count * up_count)
    cosine, sines = np.cos(angles) * factor, np.sin(angles) * factor
    same = np.eye(frame_count)
    sample_count = frame_count * up_count

    def spread(entries):
        return np.einsum("uk,tv->tukv", entries, same).reshape(sample_count, sample_count)

    table = np.block([[spread(cosine), spread(sines)], [-spread(sines), spread(cosine)]])
    table = table.astype(np.float32)
    high = table.astype(jnp.bfloat16)
    low = (table - high.astype(np.float32)).astype(jnp.bfloat16)
    return high, low


def form_kernel(me_ref, after_ref, table_ref, gain_real_ref, gain_imag_ref, real_ref, imag_ref, *refs):
    out_refs, gains_ref = refs[:-1], refs[-1]
    channels, pols, _, beams, samples = out_refs[0].shape
    for c in range(channels):
        gains_ref[0, c * pols : (c + 1) * pols] = gain_real_ref[c, 0]
        gains_ref[1, c * pols : (c + 1) * pols] = gain_imag_ref[c, 0]
    gains_real, gains_imag = gains_ref[0].T, gains_ref[1].T
    table = jnp.concatenate([table_ref[me_ref[0] ^ r] for r in range(len(out_refs))], axis=0)
    for c in range(channels):
        columns = []
        for p in range(pols):
            j = c * pols + p
            gain_real, gain_imag = gains_real[:, j : j + 1], gains_imag[:, j : j + 1]
            real = real_ref[c, 0, p].astype(jnp.float32)
            imag = imag_ref[c, 0, p].astype(jnp.float32)
            real_part = (gain_real * real - gain_imag * imag).astype(jnp.bfloat16)
            imag_part = (gain_real * imag + gain_imag * real).astype(jnp.bfloat16)
            columns.append(jnp.concatenate([real_part, imag_part], axis=0))
        calibrated = jnp.concatenate(columns, axis=1)
        formed = jnp.dot(table, calibrated, preferred_element_type=jnp.float32)
        formed = formed.astype(jnp.bfloat16)
        for p in range(pols):
            for r, out_ref in enumerate(out_refs):
                for a in range(2):
                    row = (r * 2 + a) * beams
                    out_ref[c, p, a] = formed[row : row + beams, p * samples : (p + 1) * samples]


def detect_kernel(columns, me_ref, after_ref, before_ref, high_ref, low_ref, order_ref, *refs):
    formed_refs, out_refs, (sum_ref, rows_ref) = refs[:columns], refs[columns:-2], refs[-2:]
    owners, channels, own, _ = out_refs[0].shape
    _, pols, _, beams, samples = formed_refs[0].shape
    for c in range(channels):
        for r, formed_ref in enumerate(formed_refs):
            y = me_ref[0] ^ r
            for p in range(pols):
                for a in range(2):
                    rows_ref[p, y, :, a * samples : (a + 1) * samples] = formed_ref[c, p, a]
        rows = rows_ref[...].reshape(pols * columns * beams, 2 * samples)
        spectra = jnp.dot(rows, high_ref[...], preferred_element_type=jnp.float32) + jnp.dot(
            rows, low_ref[...], preferred_element_type=jnp.float32
        )
        real, imag = [], []
        for p in range(pols):
            g = [spectra[(p * columns + y) * beams :][:beams] for y in range(columns)]
            even_sum, even_diff = g[0] + g[2], g[0] - g[2]
            odd_sum, odd_diff = g[1] + g[3], g[1] - g[3]
            zero, two = even_sum + odd_sum, even_sum - odd_sum
            dr, di = even_diff[:, :samples], even_diff[:, samples:]
            qr, qi = odd_diff[:, :samples], odd_diff[:, samples:]
            real.append([zero[:, :samples], dr + qi, two[:, :samples], dr - qi])
            imag.append([zero[:, samples:], di - qr, two[:, samples:], di + qr])
        stokes, total = [], None
        for e in range(columns):
            xr, xi, yr, yi = real[0][e], imag[0][e], real[1][e], imag[1][e]
            intensity = (xr * xr + xi * xi + yr * yr + yi * yi).astype(jnp.bfloat16)
            circular = (2.0 * (xi * yr - xr * yi)).astype(jnp.bfloat16)
            stokes.append(jnp.concatenate([intensity, circular], axis=1))
            part = intensity.astype(jnp.float32)
            total = part if total is None else total + part
        sum_ref[0, c : c + 1, :] = jnp.sum(total, axis=0, keepdims=True)
        ordered = jnp.dot(
            order_ref[...], jnp.concatenate(stokes, axis=0), preferred_element_type=jnp.float32
        )
        for d in range(owners * len(out_refs)):
            block = ordered[d * own : (d + 1) * own].astype(jnp.bfloat16)
            out_refs[d // owners][d % owners, c] = block


def flag_kernel(layout, groups, me_ref, group_ref, mask_ref, *refs):
    part_refs, chunk_refs = refs[:groups], refs[groups:-3]
    out_ref, power_ref, common_ref = refs[-3:]
    beams, width = chunk_refs[0].shape[2:]
    samples = width // 2
    channels = common_ref.shape[0]
    local = layout[-1][0] + layout[-1][1]
    sources = channels // local

    @pl.when(pl.program_id(0) == 0)
    def _():
        part = local // groups

        def place(s, carry):
            for r, part_ref in enumerate(part_refs):
                first = s * local + (me_ref[0] ^ r) * part
                common_ref[pl.ds(first, part)] = part_ref[s]
            return carry

        lax.fori_loop(0, sources, place, 0)

    def blocks(work, carry):
        refs = iter(chunk_refs)
        whole, single = [], []
        for first, size, count in layout:
            if count == 1:
                whole.append((first, size, next(refs)))
            else:
                single.extend((first, size, r, next(refs)) for r in range(count))

        def step(s, carry):
            for first, size, ref in whole:
                carry = work(carry, ref.at[s], s * local + first, size)
            return carry

        carry = lax.fori_loop(0, sources, step, carry)
        for first, size, r, ref in single:
            carry = work(carry, ref.at[0], (me_ref[1] ^ r) * local + first, size)
        return carry

    def measure(level, block_ref, channel, size):
        common = common_ref[pl.ds(channel, size)]
        cleaned = block_ref[:, :, :samples].astype(jnp.float32) - common
        squares = (cleaned * cleaned).reshape(size * beams, samples)
        high = squares.astype(jnp.bfloat16)
        low = (squares - high.astype(jnp.float32)).astype(jnp.bfloat16)
        squares = jnp.concatenate([high, low], axis=1)
        power = jnp.dot(squares, group_ref[...], preferred_element_type=jnp.float32)
        power = power.reshape(size, beams, samples)
        power_ref[pl.ds(channel, size)] = power
        return level + jnp.sum(power, axis=0)

    level = blocks(measure, jnp.zeros((beams, samples), jnp.float32))
    level = jnp.sum(level, axis=1, keepdims=True) / float(channels * samples) + epsilon
    scale = jnp.broadcast_to(0.5 / level, (beams, samples))

    def flag(carry, block_ref, channel, size):
        for c in range(size):
            row = block_ref[c].astype(jnp.float32)
            cleaned = row[:, :samples] - common_ref[channel + c]
            weight = mask_ref[channel + c] * pl.reciprocal(1.0 + power_ref[channel + c] * scale)
            where = pl.ds(pl.multiple_of((channel + c) * samples, samples), samples)
            out_ref[0, :, where] = (cleaned * weight).astype(jnp.bfloat16)
            out_ref[1, :, where] = (row[:, samples:] * weight).astype(jnp.bfloat16)
        return carry

    blocks(flag, 0)


def whole_spec(array):
    return pl.BlockSpec(array.shape, lambda *_: (0,) * array.ndim)


def form(me, after, table, gains, volts, first, per_chunk, step, groups):
    real, imag = volts
    _, _, pols, feeds, samples = real.shape
    steps = per_chunk // step
    gain_spec = pl.BlockSpec((step, 1, pols, feeds), lambda i: (first // step + i, 0, 0, 0))
    volt_spec = pl.BlockSpec(
        (step, 1, pols, feeds, samples), lambda i: (first // step + i, 0, 0, 0, 0)
    )
    beams = feeds // groups
    return pl.pallas_call(
        form_kernel,
        grid=(steps,),
        in_specs=[
            pl.BlockSpec(memory_space=pltpu.SMEM),
            pl.BlockSpec(memory_space=pl.ANY),
            whole_spec(table),
            gain_spec,
            gain_spec,
            volt_spec,
            volt_spec,
        ],
        out_specs=[pl.BlockSpec((step, pols, 2, beams, samples), lambda i: (i, 0, 0, 0, 0))]
        * groups,
        out_shape=[jax.ShapeDtypeStruct((per_chunk, pols, 2, beams, samples), jnp.bfloat16)]
        * groups,
        scratch_shapes=[pltpu.VMEM((2, 8, feeds), jnp.float32)],
        cost_estimate=pl.CostEstimate(
            flops=1000,
            bytes_accessed=1000,
            transcendentals=0,
        ),
        compiler_params=pltpu.CompilerParams(vmem_limit_bytes=60 << 20),
        name="form",
    )(me, after, table, *gains, real, imag)


def detect(me, tables, order, formed, after, step, owners, direct):
    columns = len(formed)
    per_chunk, pols, _, beams, samples = formed[0].shape
    steps = per_chunk // step
    own = columns * beams // owners
    counts = [1] * owners if direct else [owners]
    block_spec = pl.BlockSpec((step, pols, 2, beams, samples), lambda i: (i, 0, 0, 0, 0))
    return pl.pallas_call(
        functools.partial(detect_kernel, columns),
        grid=(steps,),
        in_specs=[
            pl.BlockSpec(memory_space=pltpu.SMEM),
            pl.BlockSpec(memory_space=pl.ANY),
            pl.BlockSpec(memory_space=pl.ANY),
            *[whole_spec(table) for table in tables],
            whole_spec(order),
            *[block_spec] * columns,
        ],
        out_specs=[
            *[
                pl.BlockSpec((count, step, own, 2 * samples), lambda i: (0, i, 0, 0))
                for count in counts
            ],
            pl.BlockSpec((1, step, samples), lambda i: (i, 0, 0)),
        ],
        out_shape=[
            *[
                jax.ShapeDtypeStruct((count, per_chunk, own, 2 * samples), jnp.bfloat16)
                for count in counts
            ],
            jax.ShapeDtypeStruct((steps, step, samples), jnp.float32),
        ],
        scratch_shapes=[pltpu.VMEM((pols, columns, beams, 2 * samples), jnp.bfloat16)],
        cost_estimate=pl.CostEstimate(
            flops=per_chunk * DETECT_FLOPS,
            bytes_accessed=1000,
            transcendentals=0,
        ),
        compiler_params=pltpu.CompilerParams(vmem_limit_bytes=60 << 20),
        name="detect",
    )(me, *after, *tables, order, *formed)


def soft_flag(me, owned, parts, mask, frame_count):
    own, width = owned[0][0].shape[2:]
    sizes = [one[0].shape[1] for one in owned]
    layout = [(sum(sizes[:i]), sizes[i], len(one)) for i, one in enumerate(owned)]
    owned = [block for one in owned for block in one]
    samples = width // 2
    channels = mask.shape[0]
    block = 16 if own % 16 == 0 else own
    group = np.kron(np.eye(samples // frame_count), np.ones((frame_count, frame_count)))
    group = jnp.asarray(np.concatenate([group, group]) / frame_count, jnp.bfloat16)
    return pl.pallas_call(
        functools.partial(flag_kernel, layout, len(parts)),
        grid=(own // block,),
        in_specs=[
            pl.BlockSpec(memory_space=pltpu.SMEM),
            whole_spec(group),
            whole_spec(mask),
            *[whole_spec(part) for part in parts],
            *[
                pl.BlockSpec((*one.shape[:2], block, width), lambda i: (0, 0, i, 0))
                for one in owned
            ],
        ],
        out_specs=pl.BlockSpec((2, block, channels * samples), lambda i: (0, i, 0)),
        out_shape=jax.ShapeDtypeStruct((2, own, channels * samples), jnp.bfloat16),
        scratch_shapes=[
            pltpu.VMEM((channels, block, samples), jnp.float32),
            pltpu.VMEM((channels, 1, samples), jnp.float32),
        ],
        cost_estimate=pl.CostEstimate(
            flops=channels * own * samples * samples * 4,
            bytes_accessed=channels * own * samples * 8,
            transcendentals=0,
        ),
        compiler_params=pltpu.CompilerParams(vmem_limit_bytes=60 << 20),
        name="flag",
    )(me, group, mask, *parts, *owned)


def swap(one, axis, apart):
    return lax.ppermute(one, axis, [(i, i ^ apart) for i in range(lax.axis_size(axis))])


def body(voltage_real, voltage_imag, gain_real, gain_imag, channel_mask, beam_owner):
    local, _, pols, feeds, samples = voltage_real.shape
    frame_count = samples // UP
    owners, groups = lax.axis_size("chan"), lax.axis_size("grp")
    channels = local * owners
    unit = local // sum(SHARES)
    sizes = [share * unit for share in SHARES] if local == unit * sum(SHARES) else [1] * local
    chunks = len(sizes)
    firsts = [sum(sizes[:chunk]) for chunk in range(chunks)]
    step = math.gcd(*sizes, 2)

    gains = (gain_real, gain_imag)
    mine = lax.axis_index("grp")
    table = jnp.asarray(beam_table(feeds, groups))
    near = lax.axis_index("chan")
    me = jnp.stack([mine, near]).astype(jnp.int32)
    tables = [jnp.asarray(one) for one in spectral_tables(UP, frame_count, groups)]
    slots = beam_owner.shape[1]
    wanted = beam_owner[0].reshape(owners, slots // owners)
    orders = [
        (one.reshape(slots, 1) == jnp.arange(slots, dtype=jnp.int32)).astype(jnp.bfloat16)
        for one in (wanted, wanted[near ^ jnp.arange(owners, dtype=jnp.int32)])
    ]
    mask = jnp.repeat(channel_mask.astype(jnp.float32), frame_count).reshape(channels, 1, samples)
    volts = (voltage_real, voltage_imag)
    turned, owned, sums = [], [], []
    after = me
    for chunk in range(chunks + 1):
        if chunk < chunks:
            formed = form(
                me, after, table, gains, volts, firsts[chunk], sizes[chunk], step, groups
            )
            turned.append([swap(one, "grp", r) if r else one for r, one in enumerate(formed)])
            after = formed[0]
        if chunk > 0:
            direct = chunks == len(DIRECT) and DIRECT[chunk - 1]
            before = owned[-2][-1] if len(owned) > 1 else me
            *sent, part = detect(
                me,
                tables,
                orders[direct],
                turned[chunk - 1],
                [after, before],
                step,
                owners,
                direct,
            )
            sums.append(part.reshape(sizes[chunk - 1], samples))
            after = part
            if chunk == chunks:
                common = jnp.concatenate(sums, axis=0).reshape(groups, local // groups, samples)
                parts = [common[mine ^ r] for r in range(groups)]
                common = parts[0]
                for r in range(1, groups):
                    common = common + swap(parts[r], "grp", r)
                common = common / float(feeds * groups)
                common, *sent = lax.optimization_barrier((common, *sent))
            if direct:
                owned.append([swap(one, "chan", r) if r else one for r, one in enumerate(sent)])
            else:
                owned.append([lax.all_to_all(*sent, "chan", split_axis=0, concat_axis=0, tiled=True)])
    common_piece = common.reshape(-1)
    shared = common[None]
    for bit in range(owners.bit_length() - 1):
        other = swap(shared, "chan", 1 << bit)
        low = (near >> bit) % 2 == 0
        shared = jnp.where(low, jnp.stack([shared, other]), jnp.stack([other, shared]))
        shared = shared.reshape(-1, local // groups, samples)
    shared = shared[:, :, None]
    shared = [swap(shared, "grp", r) if r else shared for r in range(groups)]
    flagged = soft_flag(me, owned, shared, mask, frame_count)
    return (flagged, common_piece)


def solution(mesh):
    in_specs = (
        P("chan", "grp", None, None, None),
        P("chan", "grp", None, None, None),
        P("chan", "grp", None, None),
        P("chan", "grp", None, None),
        P(),
        P("grp", None),
    )
    out_specs = (P(None, ("chan", "grp"), None), P(("chan", "grp")))
    return jax.shard_map(body, mesh=mesh, in_specs=in_specs, out_specs=out_specs, check_vma=False)
```
